1024 devices in a mesh: lane: 32 (over y, x_lo), section: 2 (over core), tp: 16 (over z, x_hi).
Axes of the slice: x: 8 (x_hi: 2, x_lo: 4; x = x_hi * 4 + x_lo), y: 8, z: 8, core: 2. Of those that a mesh axis runs over, the one named last changes fastest.
Arguments:
- merge_hidden: bfloat16 [16384, 5120], P('lane', 'section'), may hold values from -6 to 6
- merge_weight: bfloat16 [5120, 8192], P('section', 'tp'), may hold values from -0.25 to 0.25
- merge_bias: float32 [8192], P('tp'), may hold values from -3 to 3
- row_dest: int32 [16384], P(('lane', 'section')), may hold values from -1 to 31, as said below
- image_pos: int32 [32, 2, 32, 4], P('lane', 'section'), may hold values from -1 to 255, as said below
- text_embed: bfloat16 [16384, 8192], P(('lane', 'section'), 'tp'), may hold values from -8 to 8
- norm_gain: float32 [8192], P('tp'), may hold values from 0.25 to 1.75
- kv_weight: bfloat16 [8192, 2048], P('tp'), may hold values from -0.0625 to 0.0625
- kv_grad: bfloat16 [16384, 2048], P(('lane', 'section')), may hold values from -6 to 6
Outputs:
- key_value: bfloat16 [16384, 2048], P(('lane', 'section'), 'tp')
- embed_grad: bfloat16 [16384, 8192], P(('lane', 'section'), 'tp')
- image_grad: bfloat16 [16384, 8192], P(('lane', 'section'), 'tp')
The draws below stay inside these ranges and needn't reach their ends.
Inputs may be any that keep to these rules, and one draw needn't show every extreme that they name: `row_dest`: rows come in blocks of 256: block s of lane j is rows j * 512 + s * 256 onward. Rows of one block that go to one lane number at most 4; every block sends 4 rows to some lane, and for every s some lane receives 4 rows from block s of every lane. image_pos[l, s, j, k] is the position, among the 256 tokens of block s of lane l (tokens l * 512 + s * 256 onward), of the k-th row (in row order) that block s of lane j sends to lane l, and -1 where that block sends fewer than k + 1 rows to lane l; the positions taken in one block are distinct.
All inputs are finite; a program needn't handle non-finite values.
Results may differ from the reference program's by a relative error of at most 0.007.
Values may be sent and summed in bfloat16 or wider, within the bound.
A program may use at most 32 MiB of HBM per device.

```python
import math
from functools import partial
import jax
import jax.numpy as jnp
from jax import lax

D = 8192
VD = 5120
TOK = 512
E_DEV = 512
CAP = 4
KV2 = 2048
TOK_BLOCK = 256
ROW_BLOCK = 256
TOKENS = 16384
ROWS = 16384


def section_tables(key):
    lane_count = ROWS // E_DEV
    key_counts, key_shift, key_full, key_order, key_place = jax.random.split(key, 5)
    counts = jax.random.randint(key_counts, (lane_count, lane_count), 0, CAP + 1)
    offset_lane = jax.random.randint(key_shift, (), 0, lane_count)
    source_ids = jnp.arange(lane_count)
    counts = counts.at[source_ids, (source_ids + offset_lane) % lane_count].set(CAP)
    full_lane = jax.random.randint(key_full, (), 0, lane_count)
    counts = counts.at[:, full_lane].set(CAP)
    orders = jax.vmap(partial(jax.random.permutation, x=lane_count))(jax.random.split(key_order, lane_count))
    ordered = jnp.take_along_axis(counts, orders, axis=1)
    row_ends = jnp.cumsum(ordered, axis=1)
    row_index = jnp.arange(ROW_BLOCK)
    group_index = jnp.sum(row_index[None, :, None] >= row_ends[:, None, :], axis=2)
    picked = jnp.take_along_axis(orders, jnp.minimum(group_index, lane_count - 1), axis=1)
    row_dest = jnp.where(group_index < lane_count, picked, -1).astype(jnp.int32)
    offsets = jnp.cumsum(counts, axis=0) - counts
    position_perms = jax.vmap(partial(jax.random.permutation, x=TOK_BLOCK))(jax.random.split(key_place, lane_count))
    slot_index = jnp.arange(CAP)
    flat_index = jnp.minimum(offsets.T[:, :, None] + slot_index[None, None, :], TOK_BLOCK - 1)
    gathered = jnp.take_along_axis(position_perms, flat_index.reshape(lane_count, -1), axis=1).reshape(lane_count, lane_count, CAP)
    is_valid = slot_index[None, None, :] < counts.T[:, :, None]
    image_pos = jnp.where(is_valid, gathered, -1).astype(jnp.int32)
    return (row_dest, image_pos)


def routing_tables(key):
    section_count = TOK // TOK_BLOCK
    base = jax.random.fold_in(key, 71)
    row_dest, image_pos = jax.vmap(section_tables)(jax.random.split(base, section_count))
    return (jnp.transpose(row_dest, (1, 0, 2)).reshape(-1), jnp.transpose(image_pos, (1, 0, 2, 3)))


def draw_row_dest(key, part):
    return routing_tables(key)[0]


def draw_image_pos(key, part):
    return routing_tables(key)[1]


def draw_text_embed(key, part):
    base = jax.random.fold_in(key, 13)
    key_normal, key_rough = jax.random.split(base, 2)
    column = jnp.arange(D, dtype=jnp.float32) / (D - 1)
    rough = jax.random.uniform(key_rough, (D,), minval=0.7, maxval=1.4)
    values = jax.random.normal(key_normal, (TOKENS, D)) * 0.6 * 3.0 ** column * rough
    return jnp.clip(values, -8.0, 8.0).astype(jnp.bfloat16)


def draw_merge_weight(key, part):
    base = jax.random.fold_in(key, 29)
    key_normal, key_rough = jax.random.split(base, 2)
    column = jnp.arange(D, dtype=jnp.float32) / (D - 1)
    rough = jax.random.uniform(key_rough, (D,), minval=0.7, maxval=1.4)
    values = jax.random.normal(key_normal, (VD, D)) * 0.6 * 3.0 ** column * rough
    return jnp.clip(values / math.sqrt(VD), -0.25, 0.25).astype(jnp.bfloat16)


def level_of(rng, dims, cuts, least, largest):
    level = 1.0
    for dim, shards_of in cuts:
        steps = jax.random.uniform(jax.random.fold_in(jax.random.fold_in(rng, 6), dim), (shards_of,), jnp.float32, least / len(cuts), largest / len(cuts))
        level = level * jnp.repeat(jnp.exp(steps), dims[dim] // shards_of).reshape((-1,) + (1,) * (len(dims) - 1 - dim))
    return level


def centred(stream_key, dims, spread, limit, cuts=(), held_as=jnp.bfloat16):
    result = spread * jax.random.normal(stream_key, dims, jnp.float32)
    if cuts:
        result = result * level_of(stream_key, dims, cuts, -0.22, 0.18)
    return jnp.clip(result, -limit, limit).astype(held_as)


def setup_inputs(seed: int = 0) -> dict:
    seeds = jax.random.split(jax.random.key(seed), 10)
    return {
        "merge_hidden": centred(seeds[0], (ROWS, VD), 1.0, 6.0, ((0, 32), (1, 2))),
        "merge_weight": draw_merge_weight(jax.random.fold_in(seeds[9], 71), 0),
        "merge_bias": centred(seeds[2], (D,), 0.5, 3.0, ((0, 16),), jnp.float32),
        "row_dest": draw_row_dest(jax.random.fold_in(seeds[9], 71), 0),
        "image_pos": draw_image_pos(jax.random.fold_in(seeds[9], 71), 0),
        "text_embed": draw_text_embed(jax.random.fold_in(seeds[9], 71), 0),
        "norm_gain": jnp.clip(1.0 + 0.15 * jax.random.normal(seeds[6], (D,), jnp.float32), 0.25, 1.75),
        "kv_weight": centred(seeds[7], (D, KV2), D ** -0.5, 0.0625, ((0, 16),)),
        "kv_grad": centred(seeds[8], (TOKENS, KV2), 1.0, 6.0, ((0, 64),)),
    }


EPSILON = 1e-06

def route_targets(row_dest, image_pos):
    lane_count = image_pos.shape[0]
    section_count = image_pos.shape[1]
    block_tokens = TOK // section_count
    per_block = row_dest.reshape(lane_count, section_count, -1)
    lane_ids = jnp.arange(lane_count, dtype=jnp.int32)
    matches = (per_block[:, :, :, None] == lane_ids[None, None, None, :]).astype(jnp.int32)
    before = jnp.cumsum(matches, axis=2) - matches
    row_rank = lax.optimization_barrier(jnp.sum(before * matches, axis=3)).astype(jnp.int32)
    is_valid = per_block >= 0
    dest_lane = jnp.where(is_valid, per_block, 0).astype(jnp.int32)
    source_lane = jnp.broadcast_to(lane_ids[:, None, None], per_block.shape)
    section_ids = jnp.broadcast_to(jnp.arange(section_count, dtype=jnp.int32)[None, :, None], per_block.shape)
    position = image_pos[dest_lane, section_ids, source_lane, jnp.clip(row_rank, 0, image_pos.shape[3] - 1)]
    target = (dest_lane * TOK + section_ids * block_tokens + position).astype(jnp.int32)
    return (is_valid.reshape(-1), target.reshape(-1))

def reference(merge_hidden, merge_weight, merge_bias, row_dest, image_pos, text_embed, norm_gain, kv_weight, kv_grad):
    activated = jax.nn.gelu(merge_hidden.astype(jnp.float32), approximate=False).astype(jnp.bfloat16)
    image_rows = (jnp.dot(activated, merge_weight, preferred_element_type=jnp.float32) + merge_bias).astype(jnp.bfloat16)
    is_valid, target = route_targets(row_dest, image_pos)
    target_row = jnp.where(is_valid, target, TOKENS).astype(jnp.int32)
    stream = text_embed.at[target_row].set(image_rows, mode='drop')
    lane_count = image_pos.shape[0]

    def per_lane(operands):
        lane_rows, lane_grad = operands
        widened = lane_rows.astype(jnp.float32)
        inv_rms = lax.rsqrt(lax.optimization_barrier(jnp.mean(widened * widened, axis=1, keepdims=True)) + EPSILON)
        normed = (widened * inv_rms * norm_gain).astype(jnp.bfloat16)
        key_value = jnp.dot(normed, kv_weight, preferred_element_type=jnp.float32).astype(jnp.bfloat16)
        normed_grad = jnp.dot(lane_grad, kv_weight.T, preferred_element_type=jnp.float32)
        row_dot = lax.optimization_barrier(jnp.sum(widened * norm_gain * normed_grad, axis=1, keepdims=True))
        embed_grad = (inv_rms * norm_gain * normed_grad - widened * inv_rms ** 3 * row_dot / D).astype(jnp.bfloat16)
        return (key_value, embed_grad)
    key_value, embed_grad = lax.map(per_lane, (stream.reshape(lane_count, TOK, D), kv_grad.reshape(lane_count, TOK, KV2)))
    key_value = key_value.reshape(TOKENS, KV2)
    embed_grad = embed_grad.reshape(TOKENS, D)
    picked = embed_grad[jnp.where(is_valid, target, 0).astype(jnp.int32)]
    image_grad = jnp.where(is_valid[:, None], picked, jnp.zeros_like(picked)).astype(jnp.bfloat16)
    return (key_value, embed_grad, image_grad)
```

```python
import functools

import jax
import jax.numpy as jnp
from jax import lax
from jax.experimental import pallas as pl
from jax.experimental.pallas import tpu as pltpu
from jax.sharding import PartitionSpec as P

MESH = pl.DeviceIdType.MESH
D = 8192
EPSILON = 1e-06
LANES = 32
TPS = 16
ZS = 8
CAP = 4
SLOTS = LANES * CAP
ROWS = 256
TOKENS = 256
WIDTH = 512
HALF = TOKENS // 2
KV2 = 2048
VD_DEV = 2560
CHUNK = 512
BF16 = jnp.bfloat16
F32 = jnp.float32


def erf(x):
    x = jnp.clip(x, -3.832506856900711, 3.832506856900711)
    y = x * x
    top = 0.00022905065861350646
    for c in (0.0034082910107109506, 0.050955695062380861, 0.18520832239976145, 1.128379143519084):
        top = top * y + c
    low = -1.1791602954361697e-7
    for c in (
        0.000023547966471313185,
        0.0010179625278914885,
        0.014070470171167667,
        0.11098505178285362,
        0.49746925110067538,
        1.0,
    ):
        low = low * y + c
    return x * top / low


def gelu(x):
    return 0.5 * x * (1.0 + erf(x * 0.7071067811865476))


def iota(shape, dim):
    return lax.broadcasted_iota(jnp.int32, shape, dim)


def dot(a, b):
    return jnp.dot(a, b, preferred_element_type=F32)


def dot_t(a, b):
    return lax.dot_general(a, b, (((1,), (1,)), ((), ())), preferred_element_type=F32)


def send_slots(dest):
    lanes = iota((LANES, ROWS), 0)
    matches = lanes == dest
    ones = matches.astype(F32)
    earlier = (iota((ROWS, ROWS), 0) < iota((ROWS, ROWS), 1)).astype(F32)
    before = dot(ones.astype(BF16), earlier.astype(BF16))
    rank = jnp.sum(before * ones, axis=0, keepdims=True).astype(jnp.int32)
    slot = jnp.where(dest >= 0, dest * CAP + rank, -1)
    return (iota((SLOTS, ROWS), 0) == slot).astype(F32)


def to_chunks(rows):
    total = None
    i = iota((SLOTS * 4, SLOTS), 0)
    j = iota((SLOTS * 4, SLOTS), 1)
    for c in range(4):
        pick = (i == (j // 4) * 16 + c * 4 + j % 4).astype(F32).astype(BF16)
        part = dot(pick, rows[:, c * 128 : (c + 1) * 128])
        total = part if total is None else total + part
    return total.astype(BF16).reshape(LANES, 16, 128)


def from_chunks(chunks):
    i = iota((SLOTS, SLOTS * 4), 1)
    j = iota((SLOTS, SLOTS * 4), 0)
    flat = chunks.reshape(SLOTS * 4, 128)
    parts = []
    for c in range(4):
        pick = (i == (j // 4) * 16 + c * 4 + j % 4).astype(F32).astype(BF16)
        parts.append(dot(pick, flat))
    return jnp.concatenate(parts, axis=1).astype(BF16)


def kernel(
    hidden_hbm,
    weight_hbm,
    bias_ref,
    dest_ref,
    pos_ref,
    text_hbm,
    gain_ref,
    kvw_hbm,
    kvg_hbm,
    kv_out,
    embed_out,
    image_out,
    hidden,
    weight,
    text,
    kvw,
    kvg,
    dest_in,
    own_sum,
    part_out,
    part_in,
    grad,
    stream,
    chunk_out,
    chunk_in,
    back_out,
    back_in,
    stat_out,
    stat_in,
    xg,
    prod,
    ring_out,
    ring_in,
    cross_out,
    cross_in,
    load_sem,
    sec_send,
    sec_recv,
    lane_send,
    lane_recv,
    back_send,
    back_recv,
    stat_send,
    stat_recv,
    ring_send,
    ring_recv,
    cross_send,
    cross_recv,
):
    lane = lax.axis_index("lane")
    section = lax.axis_index("section")
    tp = lax.axis_index("tp")
    z = tp // 2
    x_hi = tp % 2
    other = 1 - section

    def load(src, dst, k):
        copy = pltpu.make_async_copy(src, dst, load_sem.at[k])
        copy.start()
        return copy

    load_own = load(hidden_hbm.at[pl.ds(section * ROWS, ROWS)], hidden.at[0], 0)
    load_weight = load(weight_hbm, weight, 1)
    load_other = load(hidden_hbm.at[pl.ds(other * ROWS, ROWS)], hidden.at[1], 2)
    load_kvw = load(kvw_hbm, kvw, 3)
    load_kvg = load(kvg_hbm, kvg, 4)
    load_text = load(text_hbm, text, 5)

    barrier = pltpu.get_barrier_semaphore()

    def greet_lane(p, _):
        pl.semaphore_signal(barrier, inc=1, device_id={"lane": (lane + p) % LANES}, device_id_type=MESH)
        return 0

    def greet_tp(p, _):
        pl.semaphore_signal(barrier, inc=1, device_id={"tp": (tp + p) % TPS}, device_id_type=MESH)
        return 0

    pl.semaphore_signal(barrier, inc=1, device_id={"section": other}, device_id_type=MESH)
    lax.fori_loop(1, LANES, greet_lane, 0)
    lax.fori_loop(1, TPS, greet_tp, 0)

    slots = send_slots(dest_ref[...])
    slots_b = slots.astype(BF16)

    def merge(block, picks):
        total = None
        for k in range(VD_DEV // CHUNK):
            cols = slice(k * CHUNK, (k + 1) * CHUNK)
            picked = dot(picks, hidden[block, :, cols])
            part = dot(gelu(picked).astype(BF16), weight[cols, :])
            total = part if total is None else total + part
        return total

    load_own.wait()
    load_weight.wait()
    own_sum[...] = merge(0, slots_b)

    pl.semaphore_wait(barrier, 1 + (LANES - 1) + (TPS - 1))
    dest_copy = pltpu.make_async_remote_copy(
        dest_ref, dest_in, sec_send.at[0], sec_recv.at[0], device_id={"section": other}, device_id_type=MESH
    )
    dest_copy.start()
    load_kvw.wait()
    load_kvg.wait()
    grad[...] = dot_t(kvg[...], kvw[...])
    dest_copy.wait_recv()
    load_other.wait()
    part_out[...] = merge(1, send_slots(dest_in[...]).astype(BF16)).astype(BF16)
    part_copy = pltpu.make_async_remote_copy(
        part_out, part_in, sec_send.at[1], sec_recv.at[1], device_id={"section": other}, device_id_type=MESH
    )
    part_copy.start()

    place = (iota((TOKENS, SLOTS), 0) == pos_ref[...]).astype(F32)
    is_image = jnp.sum(place, axis=1, keepdims=True) > 0.5
    load_text.wait()

    part_copy.wait_recv()
    image = (own_sum[...] + part_in[...].astype(F32) + bias_ref[...]).astype(BF16)

    def exchange(out_ref, in_ref, send_sem, recv_sem):
        def copy(p):
            peer = (lane + p) % LANES
            return pltpu.make_async_remote_copy(
                out_ref.at[peer],
                in_ref.at[lane],
                send_sem.at[p],
                recv_sem.at[lane],
                device_id={"lane": peer},
                device_id_type=MESH,
            )

        def start(i, _):
            copy(1 + (i + 15) % 31).start()
            return 0

        def wait_recv(p, _):
            peer = (lane + p) % LANES
            pltpu.make_async_remote_copy(
                out_ref.at[peer],
                in_ref.at[peer],
                send_sem.at[p],
                recv_sem.at[peer],
                device_id={"lane": peer},
                device_id_type=MESH,
            ).wait_recv()
            return 0

        def wait_send(p, _):
            copy(p).wait_send()
            return 0

        lax.fori_loop(0, LANES - 1, start, 0)
        in_ref[lane] = out_ref[lane]
        return (
            lambda: lax.fori_loop(1, LANES, wait_recv, 0),
            lambda: lax.fori_loop(1, LANES, wait_send, 0),
        )

    chunk_out[...] = to_chunks(image)
    lane_arrived, lane_sent = exchange(chunk_out, chunk_in, lane_send, lane_recv)
    lane_arrived()

    arrived = from_chunks(chunk_in[...])
    placed = dot(place.astype(BF16), arrived)
    wide = jnp.where(is_image, placed, text[...].astype(F32))
    stream[...] = wide
    gain = gain_ref[...]
    scaled = wide * gain
    squares = jnp.sum(wide * wide, axis=1, keepdims=True)
    dots = jnp.sum(scaled * grad[...], axis=1, keepdims=True)
    first = iota((TOKENS, 128), 1) == 0
    both = jnp.transpose(jnp.where(first, squares, dots))
    stat_out[...] = both[0:2, :]
    stat_in[tp] = both[0:2, :]

    def stat_copy(p, at):
        peer = (tp + p) % TPS
        return pltpu.make_async_remote_copy(
            stat_out,
            stat_in.at[tp if at is None else peer],
            stat_send.at[p],
            stat_recv.at[tp if at is None else peer],
            device_id={"tp": peer},
            device_id_type=MESH,
        )

    def stat_start(p, _):
        stat_copy(p, None).start()
        return 0

    def stat_wait_recv(p, _):
        stat_copy(p, "in").wait_recv()
        return 0

    def stat_wait_send(p, _):
        stat_copy(p, None).wait_send()
        return 0

    lax.fori_loop(1, TPS, stat_start, 0)
    xg[...] = scaled.astype(BF16)

    def project(o):
        block = (z + o) % ZS
        prod[o] = dot(xg[...], kvw[:, pl.ds(pl.multiple_of(block * 256, 256), 256)])

    up = ((z + 1) % ZS) * 2 + x_hi
    down = ((z + ZS - 1) % ZS) * 2 + x_hi
    blocks = ((4, 5, 6, 7), (4, 3, 2, 1), (3, 2, 1), (5, 6, 7))
    targets = (down, up, up, down)
    firsts = (True, False, True, False)

    def rows_of(chain):
        return slice(0, HALF) if firsts[chain] else slice(HALF, TOKENS)

    def ring_copy(chain, step):
        k = chain * 4 + step
        return pltpu.make_async_remote_copy(
            ring_out.at[k],
            ring_in.at[k],
            ring_send.at[k],
            ring_recv.at[k],
            device_id={"tp": targets[chain]},
            device_id_type=MESH,
        )

    ring_copies = []

    def ring_step(chain, step):
        own = prod[blocks[chain][step], rows_of(chain), :]
        if step > 0:
            ring_copy(chain, step - 1).wait_recv()
            own = own + ring_in[chain * 4 + step - 1].astype(F32)
        ring_out[chain * 4 + step] = own.astype(BF16)
        copy = ring_copy(chain, step)
        copy.start()
        ring_copies.append(copy)

    project(4)
    ring_step(0, 0)
    ring_step(1, 0)
    project(3)
    ring_step(2, 0)
    project(5)
    ring_step(3, 0)
    for o in (2, 6, 1, 7, 0):
        project(o)
    for chain in range(4):
        ring_step(chain, 1)

    lax.fori_loop(1, TPS, stat_wait_recv, 0)
    totals = jnp.sum(stat_in[...], axis=0)
    inv_row = lax.rsqrt(totals[0:1, :] / D + EPSILON)
    inv = jnp.transpose(jnp.broadcast_to(inv_row, (128, TOKENS)))
    total_dots = jnp.transpose(jnp.broadcast_to(totals[1:2, :], (128, TOKENS)))
    factor = inv * inv * inv * total_dots / D
    inv4 = jnp.concatenate([inv] * 4, axis=1)
    factor4 = jnp.concatenate([factor] * 4, axis=1)
    embed = (inv4 * gain_ref[...] * grad[...] - stream[...] * factor4).astype(BF16)
    embed_out[...] = embed
    place_t = jnp.transpose(place).astype(BF16)
    back_out[...] = to_chunks(dot(place_t, embed).astype(BF16))
    back_arrived, back_sent = exchange(back_out, back_in, back_send, back_recv)

    for chain in range(4):
        ring_step(chain, 2)
    ring_step(0, 3)
    ring_step(1, 3)

    def ring_end(chain, step):
        ring_copy(chain, step).wait_recv()
        return ring_in[chain * 4 + step].astype(F32)

    first_rows = prod[0, 0:HALF, :] + ring_end(2, 2)
    last_rows = prod[0, HALF:TOKENS, :] + ring_end(3, 2)
    first_rows = first_rows + ring_end(0, 3)
    last_rows = last_rows + ring_end(1, 3)
    summed = jnp.concatenate([first_rows, last_rows], axis=0)
    left, right = summed[:, 0:128], summed[:, 128:256]
    cross_out[...] = jnp.where(x_hi == 0, right, left).astype(BF16)
    kept = jnp.where(x_hi == 0, left, right)
    cross = pltpu.make_async_remote_copy(
        cross_out,
        cross_in,
        cross_send,
        cross_recv,
        device_id={"tp": z * 2 + (1 - x_hi)},
        device_id_type=MESH,
    )
    cross.start()

    back_arrived()
    returned = from_chunks(back_in[...])
    image_out[...] = dot(jnp.transpose(slots).astype(BF16), returned).astype(BF16)

    cross.wait_recv()
    kv_out[...] = (inv * (kept + cross_in[...].astype(F32))).astype(BF16)

    dest_copy.wait_send()
    part_copy.wait_send()
    lane_sent()
    back_sent()
    lax.fori_loop(1, TPS, stat_wait_send, 0)
    for copy in ring_copies:
        copy.wait_send()
    cross.wait_send()


def on_device(
    merge_hidden,
    merge_weight,
    merge_bias,
    row_dest,
    image_pos,
    text_embed,
    norm_gain,
    kv_weight,
    kv_grad,
):
    any_space = pl.BlockSpec(memory_space=pl.ANY)
    vmem = pl.BlockSpec(memory_space=pltpu.VMEM)
    dma = pltpu.SemaphoreType.DMA
    return pl.pallas_call(
        kernel,
        name="step",
        out_shape=(
            jax.ShapeDtypeStruct((TOKENS, KV2 // TPS), BF16),
            jax.ShapeDtypeStruct((TOKENS, WIDTH), BF16),
            jax.ShapeDtypeStruct((ROWS, WIDTH), BF16),
        ),
        in_specs=[any_space, any_space, vmem, vmem, vmem, any_space, vmem, any_space, any_space],
        out_specs=(vmem, vmem, vmem),
        scratch_shapes=[
            pltpu.VMEM((2, ROWS, VD_DEV), BF16),
            pltpu.VMEM((VD_DEV, WIDTH), BF16),
            pltpu.VMEM((TOKENS, WIDTH), BF16),
            pltpu.VMEM((WIDTH, KV2), BF16),
            pltpu.VMEM((TOKENS, KV2), BF16),
            pltpu.VMEM((1, ROWS), jnp.int32),
            pltpu.VMEM((SLOTS, WIDTH), F32),
            pltpu.VMEM((SLOTS, WIDTH), BF16),
            pltpu.VMEM((SLOTS, WIDTH), BF16),
            pltpu.VMEM((TOKENS, WIDTH), F32),
            pltpu.VMEM((TOKENS, WIDTH), F32),
            pltpu.VMEM((LANES, 16, 128), BF16),
            pltpu.VMEM((LANES, 16, 128), BF16),
            pltpu.VMEM((LANES, 16, 128), BF16),
            pltpu.VMEM((LANES, 16, 128), BF16),
            pltpu.VMEM((2, TOKENS), F32),
            pltpu.VMEM((TPS, 2, TOKENS), F32),
            pltpu.VMEM((TOKENS, WIDTH), BF16),
            pltpu.VMEM((ZS, TOKENS, 256), F32),
            pltpu.VMEM((16, HALF, 256), BF16),
            pltpu.VMEM((16, HALF, 256), BF16),
            pltpu.VMEM((TOKENS, 128), BF16),
            pltpu.VMEM((TOKENS, 128), BF16),
            dma((6,)),
            dma((2,)),
            dma((2,)),
            dma((LANES,)),
            dma((LANES,)),
            dma((LANES,)),
            dma((LANES,)),
            dma((TPS,)),
            dma((TPS,)),
            dma((16,)),
            dma((16,)),
            pltpu.SemaphoreType.DMA,
            pltpu.SemaphoreType.DMA,
        ],
        compiler_params=pltpu.CompilerParams(
            collective_id=0, has_side_effects=True, vmem_limit_bytes=60 * 1024 * 1024
        ),
    )(
        merge_hidden,
        merge_weight,
        merge_bias.reshape(1, WIDTH),
        row_dest.reshape(1, ROWS),
        image_pos.reshape(1, SLOTS),
        text_embed,
        norm_gain.reshape(1, WIDTH),
        kv_weight,
        kv_grad,
    )


def solution(mesh):
    in_specs = (
        P("lane", "section"),
        P("section", "tp"),
        P("tp"),
        P(("lane", "section")),
        P("lane", "section", None, None),
        P(("lane", "section"), "tp"),
        P("tp"),
        P("tp", None),
        P(("lane", "section"), None),
    )
    out_specs = (
        P(("lane", "section"), "tp"),
        P(("lane", "section"), "tp"),
        P(("lane", "section"), "tp"),
    )
    return jax.shard_map(on_device, mesh=mesh, in_specs=in_specs, out_specs=out_specs, check_vma=False)
```

```python
import functools

import jax
import jax.numpy as jnp
from jax import lax
from jax.experimental import pallas as pl
from jax.experimental.pallas import tpu as pltpu
from jax.sharding import PartitionSpec as P

MESH = pl.DeviceIdType.MESH
D = 8192
EPSILON = 1e-06
LANES = 32
TPS = 16
ZS = 8
CAP = 4
SLOTS = LANES * CAP
ROWS = 256
TOKENS = 256
WIDTH = 512
HALF = TOKENS // 2
KV2 = 2048
VD_DEV = 2560
CHUNK = 512
BF16 = jnp.bfloat16
F32 = jnp.float32


def erf(x):
    x = jnp.clip(x, -3.832506856900711, 3.832506856900711)
    y = x * x
    top = 0.00022905065861350646
    for c in (0.0034082910107109506, 0.050955695062380861, 0.18520832239976145, 1.128379143519084):
        top = top * y + c
    low = -1.1791602954361697e-7
    for c in (
        0.000023547966471313185,
        0.0010179625278914885,
        0.014070470171167667,
        0.11098505178285362,
        0.49746925110067538,
        1.0,
    ):
        low = low * y + c
    return x * top / low


def gelu(x):
    return 0.5 * x * (1.0 + erf(x * 0.7071067811865476))


def iota(shape, dim):
    return lax.broadcasted_iota(jnp.int32, shape, dim)


def dot(a, b):
    return jnp.dot(a, b, preferred_element_type=F32)


def dot_t(a, b):
    return lax.dot_general(a, b, (((1,), (1,)), ((), ())), preferred_element_type=F32)


def send_slots(dest):
    lanes = iota((LANES, ROWS), 0)
    matches = lanes == dest
    ones = matches.astype(F32)
    earlier = (iota((ROWS, ROWS), 0) < iota((ROWS, ROWS), 1)).astype(F32)
    before = dot(ones.astype(BF16), earlier.astype(BF16))
    rank = jnp.sum(before * ones, axis=0, keepdims=True).astype(jnp.int32)
    slot = jnp.where(dest >= 0, dest * CAP + rank, -1)
    return (iota((SLOTS, ROWS), 0) == slot).astype(F32)


def to_chunks(rows):
    total = None
    i = iota((SLOTS * 4, SLOTS), 0)
    j = iota((SLOTS * 4, SLOTS), 1)
    for c in range(4):
        pick = (i == (j // 4) * 16 + c * 4 + j % 4).astype(F32).astype(BF16)
        part = dot(pick, rows[:, c * 128 : (c + 1) * 128])
        total = part if total is None else total + part
    return total.astype(BF16).reshape(LANES, 16, 128)


def from_chunks(chunks):
    i = iota((SLOTS, SLOTS * 4), 1)
    j = iota((SLOTS, SLOTS * 4), 0)
    flat = chunks.reshape(SLOTS * 4, 128)
    parts = []
    for c in range(4):
        pick = (i == (j // 4) * 16 + c * 4 + j % 4).astype(F32).astype(BF16)
        parts.append(dot(pick, flat))
    return jnp.concatenate(parts, axis=1).astype(BF16)


def kernel(
    hidden_hbm,
    weight_hbm,
    bias_hbm,
    dest_hbm,
    pos_hbm,
    text_hbm,
    gain_hbm,
    kvw_hbm,
    kvg_hbm,
    kv_out,
    embed_out,
    image_out,
    hidden,
    weight,
    bias_ref,
    dest_ref,
    pos_ref,
    text,
    gain_ref,
    kvw,
    kvg,
    own_sum,
    part_out,
    part_in,
    grad,
    stream,
    chunk_out,
    chunk_in,
    back_out,
    back_in,
    stat_out,
    stat_in,
    xg,
    prod,
    ring_out,
    ring_in,
    slot_xg,
    slot_prod,
    slot_out,
    slot_in,
    cross_out,
    cross_in,
    slot_cross_out,
    slot_cross_in,
    load_sem,
    sec_send,
    sec_recv,
    lane_send,
    lane_recv,
    back_send,
    back_recv,
    stat_send,
    stat_recv,
    ring_send,
    ring_recv,
    slot_send,
    slot_recv,
    cross_send,
    cross_recv,
):
    lane = lax.axis_index("lane")
    section = lax.axis_index("section")
    tp = lax.axis_index("tp")
    z = tp // 2
    x_hi = tp % 2
    other = 1 - section

    barrier = pltpu.get_barrier_semaphore()

    def greet_lane(i, _):
        p = 1 + (i + 15) % 31
        pl.semaphore_signal(barrier, inc=1, device_id={"lane": (lane + p) % LANES}, device_id_type=MESH)
        return 0

    def greet_tp(i, _):
        p = 1 + (i + 7) % 15
        pl.semaphore_signal(barrier, inc=1, device_id={"tp": (tp + p) % TPS}, device_id_type=MESH)
        return 0

    def load(src, dst, k):
        copy = pltpu.make_async_copy(src, dst, load_sem.at[k])
        copy.start()
        return copy

    load_dest = load(dest_hbm, dest_ref, 0)
    load_own = load(hidden_hbm.at[pl.ds(section * ROWS, ROWS)], hidden.at[0], 1)
    load_weight = load(weight_hbm, weight, 2)
    lax.fori_loop(0, LANES - 1, greet_lane, 0)
    lax.fori_loop(0, TPS - 1, greet_tp, 0)
    pl.semaphore_signal(barrier, inc=1, device_id={"section": other}, device_id_type=MESH)
    load_other = load(hidden_hbm.at[pl.ds(other * ROWS, ROWS)], hidden.at[1], 3)
    load_pos = load(pos_hbm, pos_ref, 4)
    load_gain = load(gain_hbm, gain_ref, 5)
    load_bias = load(bias_hbm, bias_ref, 6)
    load_text = load(text_hbm, text, 7)
    load_kvw = load(kvw_hbm, kvw, 8)
    load_kvg = load(kvg_hbm, kvg, 9)

    load_dest.wait()
    slots = send_slots(dest_ref[...])
    slots_b = slots.astype(BF16)
    load_own.wait()
    load_weight.wait()
    total = None
    for k in range(VD_DEV // CHUNK):
        cols = slice(k * CHUNK, (k + 1) * CHUNK)
        picked = dot(slots_b, hidden[0, :, cols])
        part = dot(gelu(picked).astype(BF16), weight[cols, :])
        total = part if total is None else total + part
    own_sum[...] = total

    load_other.wait()
    for half in range(2):
        rows = slice(half * HALF, (half + 1) * HALF)
        total = None
        for k in range(VD_DEV // CHUNK):
            cols = slice(k * CHUNK, (k + 1) * CHUNK)
            wide = hidden[1, rows, cols].astype(F32)
            part = dot(gelu(wide).astype(BF16), weight[cols, :])
            total = part if total is None else total + part
        part_out[rows, :] = total.astype(BF16)

    load_pos.wait()
    spread = (iota((LANES, SLOTS), 1) // CAP == iota((LANES, SLOTS), 0)).astype(F32)
    pos_all = dot(pos_ref[...].astype(F32).astype(BF16), spread.astype(BF16))
    pos_own = iota((CAP, SLOTS), 1) % CAP == iota((CAP, SLOTS), 0)
    pos = jnp.sum(jnp.where(pos_own, pos_all, 0.0), axis=0, keepdims=True)
    place = (iota((TOKENS, SLOTS), 0) == pos.astype(jnp.int32)).astype(F32)
    is_image = jnp.sum(place, axis=1, keepdims=True) > 0.5

    load_gain.wait()
    load_bias.wait()
    load_text.wait()
    load_kvw.wait()
    gain = gain_ref[...]
    xg[...] = jnp.where(is_image, 0.0, text[...].astype(F32) * gain).astype(BF16)

    def columns(o):
        block = (z + o) % ZS
        return kvw[:, pl.ds(pl.multiple_of(block * 256, 256), 256)]

    def project(o):
        prod[o] = dot(xg[...], columns(o))

    up = ((z + 1) % ZS) * 2 + x_hi
    down = ((z + ZS - 1) % ZS) * 2 + x_hi
    blocks = ((4, 5, 6, 7), (4, 3, 2, 1), (3, 2, 1), (5, 6, 7))
    targets = (down, up, up, down)
    firsts = (True, False, True, False)

    def ring(out_ref, in_ref, send_sem, recv_sem, prod_ref, half):
        started = []

        def copy_of(chain, step):
            k = chain * 4 + step
            return pltpu.make_async_remote_copy(
                out_ref.at[k],
                in_ref.at[k],
                send_sem.at[k],
                recv_sem.at[k],
                device_id={"tp": targets[chain]},
                device_id_type=MESH,
            )

        def step_of(chain, step):
            rows = slice(0, half) if firsts[chain] else slice(half, 2 * half)
            own = prod_ref[blocks[chain][step], rows, :]
            if step > 0:
                copy_of(chain, step - 1).wait_recv()
                own = own + in_ref[chain * 4 + step - 1].astype(F32)
            out_ref[chain * 4 + step] = own.astype(BF16)
            copy = copy_of(chain, step)
            copy.start()
            started.append(copy)

        def arrived_at(chain, step):
            copy_of(chain, step).wait_recv()
            return in_ref[chain * 4 + step].astype(F32)

        def end():
            first_rows = prod_ref[0, 0:half, :] + arrived_at(2, 2)
            last_rows = prod_ref[0, half : 2 * half, :] + arrived_at(3, 2)
            first_rows = first_rows + arrived_at(0, 3)
            last_rows = last_rows + arrived_at(1, 3)
            summed = jnp.concatenate([first_rows, last_rows], axis=0)
            left, right = summed[:, 0:128], summed[:, 128:256]
            return jnp.where(x_hi == 0, left, right), jnp.where(x_hi == 0, right, left)

        def sent():
            for copy in started:
                copy.wait_send()

        return step_of, end, sent

    text_step, text_end, text_sent = ring(ring_out, ring_in, ring_send, ring_recv, prod, HALF)
    slot_step, slot_end, slot_sent = ring(slot_out, slot_in, slot_send, slot_recv, slot_prod, SLOTS // 2)

    project(4)
    project(3)
    project(5)

    pl.semaphore_wait(barrier, 1 + (LANES - 1) + (TPS - 1))
    part_copy = pltpu.make_async_remote_copy(
        part_out, part_in, sec_send, sec_recv, device_id={"section": other}, device_id_type=MESH
    )
    part_copy.start()
    for chain in range(4):
        text_step(chain, 0)
    for o in (2, 6, 1, 7, 0):
        project(o)
    load_kvg.wait()
    grad[...] = dot_t(kvg[...], kvw[...])

    part_copy.wait_recv()
    image = (own_sum[...] + dot(slots_b, part_in[...]) + bias_ref[...]).astype(BF16)

    def exchange(out_ref, in_ref, send_sem, recv_sem):
        def copy(p):
            peer = (lane + p) % LANES
            return pltpu.make_async_remote_copy(
                out_ref.at[peer],
                in_ref.at[lane],
                send_sem.at[p],
                recv_sem.at[lane],
                device_id={"lane": peer},
                device_id_type=MESH,
            )

        def start(i, _):
            copy(1 + (i + 15) % 31).start()
            return 0

        def wait_recv(p, _):
            peer = (lane + p) % LANES
            pltpu.make_async_remote_copy(
                out_ref.at[peer],
                in_ref.at[peer],
                send_sem.at[p],
                recv_sem.at[peer],
                device_id={"lane": peer},
                device_id_type=MESH,
            ).wait_recv()
            return 0

        def wait_send(p, _):
            copy(p).wait_send()
            return 0

        lax.fori_loop(0, LANES - 1, start, 0)
        in_ref[lane] = out_ref[lane]
        return (
            lambda: lax.fori_loop(1, LANES, wait_recv, 0),
            lambda: lax.fori_loop(1, LANES, wait_send, 0),
        )

    chunk_out[...] = to_chunks(image)
    lane_arrived, lane_sent = exchange(chunk_out, chunk_in, lane_send, lane_recv)

    for chain in range(4):
        text_step(chain, 1)
    for chain in range(4):
        if len(blocks[chain]) > 2:
            text_step(chain, 2)

    lane_arrived()
    arrived = from_chunks(chunk_in[...])
    placed = dot(place.astype(BF16), arrived)
    wide = jnp.where(is_image, placed, text[...].astype(F32))
    stream[...] = wide
    squares = jnp.sum(wide * wide, axis=1, keepdims=True)
    dots = jnp.sum(wide * gain * grad[...], axis=1, keepdims=True)
    first = iota((TOKENS, 128), 1) == 0
    both = jnp.transpose(jnp.where(first, squares, dots))
    stat_out[...] = both[0:2, :]
    stat_in[tp] = both[0:2, :]

    def stat_copy(p, at):
        peer = (tp + p) % TPS
        return pltpu.make_async_remote_copy(
            stat_out,
            stat_in.at[tp if at is None else peer],
            stat_send.at[p],
            stat_recv.at[tp if at is None else peer],
            device_id={"tp": peer},
            device_id_type=MESH,
        )

    def stat_start(i, _):
        stat_copy(1 + (i + 7) % 15, None).start()
        return 0

    def stat_wait_recv(p, _):
        stat_copy(p, "in").wait_recv()
        return 0

    def stat_wait_send(p, _):
        stat_copy(p, None).wait_send()
        return 0

    lax.fori_loop(0, TPS - 1, stat_start, 0)
    slot_xg[...] = (arrived.astype(F32) * gain).astype(BF16)

    def slot_project(o):
        slot_prod[o] = dot(slot_xg[...], columns(o))

    slot_project(4)
    slot_step(0, 0)
    slot_step(1, 0)
    slot_project(3)
    slot_step(2, 0)
    slot_project(5)
    slot_step(3, 0)
    text_step(0, 3)
    text_step(1, 3)
    for o in (2, 6, 1, 7, 0):
        slot_project(o)
    for chain in range(4):
        slot_step(chain, 1)

    def cross_copy(out_ref, in_ref, k):
        return pltpu.make_async_remote_copy(
            out_ref,
            in_ref,
            cross_send.at[k],
            cross_recv.at[k],
            device_id={"tp": z * 2 + (1 - x_hi)},
            device_id_type=MESH,
        )

    text_kept, text_away = text_end()
    cross_out[...] = text_away.astype(BF16)
    text_cross = cross_copy(cross_out, cross_in, 0)
    text_cross.start()

    lax.fori_loop(1, TPS, stat_wait_recv, 0)
    totals = jnp.sum(stat_in[...], axis=0)
    inv_row = lax.rsqrt(totals[0:1, :] / D + EPSILON)
    inv = jnp.transpose(jnp.broadcast_to(inv_row, (128, TOKENS)))
    total_dots = jnp.transpose(jnp.broadcast_to(totals[1:2, :], (128, TOKENS)))
    factor = inv * inv * inv * total_dots / D
    inv4 = jnp.concatenate([inv] * 4, axis=1)
    factor4 = jnp.concatenate([factor] * 4, axis=1)
    embed = (inv4 * gain * grad[...] - stream[...] * factor4).astype(BF16)
    embed_out[...] = embed
    place_t = jnp.transpose(place).astype(BF16)
    back_out[...] = to_chunks(dot(place_t, embed).astype(BF16))
    back_arrived, back_sent = exchange(back_out, back_in, back_send, back_recv)

    for chain in range(4):
        if len(blocks[chain]) > 2:
            slot_step(chain, 2)
    slot_step(0, 3)
    slot_step(1, 3)
    slot_kept, slot_away = slot_end()
    slot_cross_out[...] = slot_away.astype(BF16)
    slot_cross = cross_copy(slot_cross_out, slot_cross_in, 1)
    slot_cross.start()

    back_arrived()
    returned = from_chunks(back_in[...])
    image_out[...] = dot(jnp.transpose(slots).astype(BF16), returned).astype(BF16)

    text_cross.wait_recv()
    text_sum = text_kept + cross_in[...].astype(F32)
    slot_cross.wait_recv()
    slot_sum = slot_kept + slot_cross_in[...].astype(F32)
    high = slot_sum.astype(BF16)
    low = (slot_sum - high.astype(F32)).astype(BF16)
    place_b = place.astype(BF16)
    slot_placed = dot(place_b, high) + dot(place_b, low)
    kv_out[...] = (inv * jnp.where(is_image, slot_placed, text_sum)).astype(BF16)

    part_copy.wait_send()
    lane_sent()
    back_sent()
    lax.fori_loop(1, TPS, stat_wait_send, 0)
    text_sent()
    slot_sent()
    text_cross.wait_send()
    slot_cross.wait_send()


def finish(kv, embed, image, kv_hbm, embed_hbm, image_hbm, sems):
    copies = []
    for k, (src, dst) in enumerate(((embed, embed_hbm), (image, image_hbm), (kv, kv_hbm))):
        copy = pltpu.make_async_copy(src, dst, sems.at[k])
        copy.start()
        copies.append(copy)
    for copy in copies:
        copy.wait()


def on_device(
    merge_hidden,
    merge_weight,
    merge_bias,
    row_dest,
    image_pos,
    text_embed,
    norm_gain,
    kv_weight,
    kv_grad,
):
    any_space = pl.BlockSpec(memory_space=pl.ANY)
    vmem = pl.BlockSpec(memory_space=pltpu.VMEM)
    dma = pltpu.SemaphoreType.DMA
    shapes = ((TOKENS, KV2 // TPS), (TOKENS, WIDTH), (ROWS, WIDTH))
    results = pl.pallas_call(
        kernel,
        name="step",
        out_shape=tuple(pltpu.VMEM(shape, BF16) for shape in shapes),
        in_specs=[any_space] * 9,
        out_specs=(vmem, vmem, vmem),
        scratch_shapes=[
            pltpu.VMEM((2, ROWS, VD_DEV), BF16),
            pltpu.VMEM((VD_DEV, WIDTH), BF16),
            pltpu.VMEM((1, WIDTH), F32),
            pltpu.VMEM((1, ROWS), jnp.int32),
            pltpu.VMEM((CAP, LANES), jnp.int32),
            pltpu.VMEM((TOKENS, WIDTH), BF16),
            pltpu.VMEM((1, WIDTH), F32),
            pltpu.VMEM((WIDTH, KV2), BF16),
            pltpu.VMEM((TOKENS, KV2), BF16),
            pltpu.VMEM((SLOTS, WIDTH), F32),
            pltpu.VMEM((ROWS, WIDTH), BF16),
            pltpu.VMEM((ROWS, WIDTH), BF16),
            pltpu.VMEM((TOKENS, WIDTH), F32),
            pltpu.VMEM((TOKENS, WIDTH), F32),
            pltpu.VMEM((LANES, 16, 128), BF16),
            pltpu.VMEM((LANES, 16, 128), BF16),
            pltpu.VMEM((LANES, 16, 128), BF16),
            pltpu.VMEM((LANES, 16, 128), BF16),
            pltpu.VMEM((2, TOKENS), F32),
            pltpu.VMEM((TPS, 2, TOKENS), F32),
            pltpu.VMEM((TOKENS, WIDTH), BF16),
            pltpu.VMEM((ZS, TOKENS, 256), F32),
            pltpu.VMEM((16, HALF, 256), BF16),
            pltpu.VMEM((16, HALF, 256), BF16),
            pltpu.VMEM((SLOTS, WIDTH), BF16),
            pltpu.VMEM((ZS, SLOTS, 256), F32),
            pltpu.VMEM((16, SLOTS // 2, 256), BF16),
            pltpu.VMEM((16, SLOTS // 2, 256), BF16),
            pltpu.VMEM((TOKENS, 128), BF16),
            pltpu.VMEM((TOKENS, 128), BF16),
            pltpu.VMEM((SLOTS, 128), BF16),
            pltpu.VMEM((SLOTS, 128), BF16),
            dma((10,)),
            pltpu.SemaphoreType.DMA,
            pltpu.SemaphoreType.DMA,
            dma((LANES,)),
            dma((LANES,)),
            dma((LANES,)),
            dma((LANES,)),
            dma((TPS,)),
            dma((TPS,)),
            dma((16,)),
            dma((16,)),
            dma((16,)),
            dma((16,)),
            dma((2,)),
            dma((2,)),
        ],
        compiler_params=pltpu.CompilerParams(
            collective_id=0, has_side_effects=True, vmem_limit_bytes=65011712
        ),
    )(
        merge_hidden,
        merge_weight,
        merge_bias.reshape(1, WIDTH),
        row_dest.reshape(1, ROWS),
        jnp.transpose(image_pos.reshape(LANES, CAP)),
        text_embed,
        norm_gain.reshape(1, WIDTH),
        kv_weight,
        kv_grad,
    )
    return pl.pallas_call(
        finish,
        name="finish",
        out_shape=tuple(jax.ShapeDtypeStruct(shape, BF16) for shape in shapes),
        in_specs=[vmem] * 3,
        out_specs=(any_space,) * 3,
        scratch_shapes=[dma((3,))],
        compiler_params=pltpu.CompilerParams(vmem_limit_bytes=4 * 1024 * 1024),
    )(*results)


def solution(mesh):
    in_specs = (
        P("lane", "section"),
        P("section", "tp"),
        P("tp"),
        P(("lane", "section")),
        P("lane", "section", None, None),
        P(("lane", "section"), "tp"),
        P("tp"),
        P("tp", None),
        P(("lane", "section"), None),
    )
    out_specs = (
        P(("lane", "section"), "tp"),
        P(("lane", "section"), "tp"),
        P(("lane", "section"), "tp"),
    )
    return jax.shard_map(on_device, mesh=mesh, in_specs=in_specs, out_specs=out_specs, check_vma=False)
```

```python
import functools

import jax
import jax.numpy as jnp
from jax import lax
from jax.experimental import pallas as pl
from jax.experimental.pallas import tpu as pltpu
from jax.sharding import PartitionSpec as P

MESH = pl.DeviceIdType.MESH
D = 8192
EPSILON = 1e-06
LANES = 32
TPS = 16
ZS = 8
CAP = 4
SLOTS = LANES * CAP
ROWS = 256
TOKENS = 256
WIDTH = 512
HALF = TOKENS // 2
KV2 = 2048
VD_DEV = 2560
CHUNK = 512
BF16 = jnp.bfloat16
F32 = jnp.float32


def erf(x):
    x = jnp.clip(x, -3.832506856900711, 3.832506856900711)
    y = x * x
    top = 0.00022905065861350646
    for c in (0.0034082910107109506, 0.050955695062380861, 0.18520832239976145, 1.128379143519084):
        top = top * y + c
    low = -1.1791602954361697e-7
    for c in (
        0.000023547966471313185,
        0.0010179625278914885,
        0.014070470171167667,
        0.11098505178285362,
        0.49746925110067538,
        1.0,
    ):
        low = low * y + c
    return x * top / low


def gelu(x):
    return 0.5 * x * (1.0 + erf(x * 0.7071067811865476))


def iota(shape, dim):
    return lax.broadcasted_iota(jnp.int32, shape, dim)


def dot(a, b):
    return jnp.dot(a, b, preferred_element_type=F32)


def dot_t(a, b):
    return lax.dot_general(a, b, (((1,), (1,)), ((), ())), preferred_element_type=F32)


def send_slots(dest):
    lanes = iota((LANES, ROWS), 0)
    matches = lanes == dest
    ones = matches.astype(F32)
    earlier = (iota((ROWS, ROWS), 0) < iota((ROWS, ROWS), 1)).astype(F32)
    before = dot(ones.astype(BF16), earlier.astype(BF16))
    rank = jnp.sum(before * ones, axis=0, keepdims=True).astype(jnp.int32)
    slot = jnp.where(dest >= 0, dest * CAP + rank, -1)
    return (iota((SLOTS, ROWS), 0) == slot).astype(F32)


def to_chunks(rows):
    total = None
    i = iota((SLOTS * 4, SLOTS), 0)
    j = iota((SLOTS * 4, SLOTS), 1)
    for c in range(4):
        pick = (i == (j // 4) * 16 + c * 4 + j % 4).astype(F32).astype(BF16)
        part = dot(pick, rows[:, c * 128 : (c + 1) * 128])
        total = part if total is None else total + part
    return total.astype(BF16).reshape(LANES, 16, 128)


def from_chunks(chunks):
    i = iota((SLOTS, SLOTS * 4), 1)
    j = iota((SLOTS, SLOTS * 4), 0)
    flat = chunks.reshape(SLOTS * 4, 128)
    parts = []
    for c in range(4):
        pick = (i == (j // 4) * 16 + c * 4 + j % 4).astype(F32).astype(BF16)
        parts.append(dot(pick, flat))
    return jnp.concatenate(parts, axis=1).astype(BF16)


def kernel(
    hidden_hbm,
    weight_hbm,
    bias_hbm,
    dest_hbm,
    pos_hbm,
    text_hbm,
    gain_hbm,
    kvw_hbm,
    kvg_hbm,
    kv_out,
    embed_out,
    image_out,
    hidden,
    weight,
    bias_ref,
    dest_ref,
    pos_ref,
    text,
    gain_ref,
    kvw,
    kvg,
    own_sum,
    part_out,
    part_in,
    grad,
    stream,
    chunk_out,
    chunk_in,
    back_out,
    back_in,
    stat_out,
    stat_in,
    xg,
    prod,
    ring_out,
    ring_in,
    slot_xg,
    slot_prod,
    slot_out,
    slot_in,
    cross_out,
    cross_in,
    end_out,
    end_in,
    load_sem,
    sec_send,
    sec_recv,
    lane_send,
    lane_recv,
    back_send,
    back_recv,
    stat_send,
    stat_recv,
    ring_send,
    ring_recv,
    slot_send,
    slot_recv,
    end_send,
    end_recv,
    cross_send,
    cross_recv,
):
    lane = lax.axis_index("lane")
    section = lax.axis_index("section")
    tp = lax.axis_index("tp")
    z = tp // 2
    x_hi = tp % 2
    other = 1 - section

    barrier = pltpu.get_barrier_semaphore()

    def greet_lane(i, _):
        p = 1 + (i + 15) % 31
        pl.semaphore_signal(barrier, inc=1, device_id={"lane": (lane + p) % LANES}, device_id_type=MESH)
        return 0

    def greet_tp(i, _):
        p = 1 + (i + 7) % 15
        pl.semaphore_signal(barrier, inc=1, device_id={"tp": (tp + p) % TPS}, device_id_type=MESH)
        return 0

    def load(src, dst, k):
        copy = pltpu.make_async_copy(src, dst, load_sem.at[k])
        copy.start()
        return copy

    load_dest = load(dest_hbm, dest_ref, 0)
    load_own = load(hidden_hbm.at[pl.ds(section * ROWS, ROWS)], hidden.at[0], 1)
    load_weight = load(weight_hbm, weight, 2)
    lax.fori_loop(0, LANES - 1, greet_lane, 0, unroll=True)
    lax.fori_loop(0, TPS - 1, greet_tp, 0, unroll=True)
    pl.semaphore_signal(barrier, inc=1, device_id={"section": other}, device_id_type=MESH)
    load_other = load(hidden_hbm.at[pl.ds(other * ROWS, ROWS)], hidden.at[1], 3)
    load_pos = load(pos_hbm, pos_ref, 4)
    load_gain = load(gain_hbm, gain_ref, 5)
    load_bias = load(bias_hbm, bias_ref, 6)
    load_text = load(text_hbm, text, 7)
    load_kvw = load(kvw_hbm, kvw, 8)
    load_kvg = load(kvg_hbm, kvg, 9)

    load_dest.wait()
    slots = send_slots(dest_ref[...])
    slots_b = slots.astype(BF16)
    load_own.wait()
    load_weight.wait()
    total = None
    for k in range(VD_DEV // CHUNK):
        cols = slice(k * CHUNK, (k + 1) * CHUNK)
        picked = dot(slots_b, hidden[0, :, cols])
        part = dot(gelu(picked).astype(BF16), weight[cols, :])
        total = part if total is None else total + part
    own_sum[...] = total

    load_other.wait()
    for half in range(2):
        rows = slice(half * HALF, (half + 1) * HALF)
        total = None
        for k in range(VD_DEV // CHUNK):
            cols = slice(k * CHUNK, (k + 1) * CHUNK)
            wide = hidden[1, rows, cols].astype(F32)
            part = dot(gelu(wide).astype(BF16), weight[cols, :])
            total = part if total is None else total + part
        part_out[rows, :] = total.astype(BF16)

    pl.semaphore_wait(barrier, 1 + (LANES - 1) + (TPS - 1))
    part_copy = pltpu.make_async_remote_copy(
        part_out, part_in, sec_send, sec_recv, device_id={"section": other}, device_id_type=MESH
    )
    part_copy.start()
    load_pos.wait()
    spread = (iota((LANES, SLOTS), 1) // CAP == iota((LANES, SLOTS), 0)).astype(F32)
    pos_all = dot(pos_ref[...].astype(F32).astype(BF16), spread.astype(BF16))
    pos_own = iota((CAP, SLOTS), 1) % CAP == iota((CAP, SLOTS), 0)
    pos = jnp.sum(jnp.where(pos_own, pos_all, 0.0), axis=0, keepdims=True)
    place = (iota((TOKENS, SLOTS), 0) == pos.astype(jnp.int32)).astype(F32)
    is_image = jnp.sum(place, axis=1, keepdims=True) > 0.5

    load_gain.wait()
    load_bias.wait()
    load_text.wait()
    load_kvw.wait()
    gain = gain_ref[...]
    xg[...] = jnp.where(is_image, 0.0, text[...].astype(F32) * gain).astype(BF16)

    def columns(o):
        block = (z + o) % ZS
        return kvw[:, pl.ds(pl.multiple_of(block * 256, 256), 256)]

    def project(o):
        prod[o] = dot(xg[...], columns(o))

    up = ((z + 1) % ZS) * 2 + x_hi
    down = ((z + ZS - 1) % ZS) * 2 + x_hi
    blocks = ((4, 5, 6, 7), (4, 3, 2, 1), (3, 2, 1), (5, 6, 7))
    targets = (down, up, up, down)
    firsts = (True, False, True, False)

    def ring(out_ref, in_ref, send_sem, recv_sem, prod_ref, half, offsets):
        def copy_of(chain, step):
            k = offsets[chain] + step
            return pltpu.make_async_remote_copy(
                out_ref.at[k],
                in_ref.at[k],
                send_sem,
                recv_sem.at[k],
                device_id={"tp": targets[chain]},
                device_id_type=MESH,
            )

        def sum_at(chain, step):
            rows = slice(0, half) if firsts[chain] else slice(half, 2 * half)
            own = prod_ref[blocks[chain][step], rows, :]
            if step > 0:
                copy_of(chain, step - 1).wait_recv()
                own = own + in_ref[offsets[chain] + step - 1].astype(F32)
            return own

        def step_of(chain, step):
            out_ref[offsets[chain] + step] = sum_at(chain, step).astype(BF16)
            copy_of(chain, step).start()

        def arrived_at(chain, step):
            copy_of(chain, step).wait_recv()
            return in_ref[offsets[chain] + step].astype(F32)

        return step_of, sum_at, arrived_at

    def own_side(block):
        left, right = block[:, 0:128], block[:, 128:256]
        return jnp.where(x_hi == 0, left, right), jnp.where(x_hi == 0, right, left)

    text_step, _, text_arrived = ring(ring_out, ring_in, ring_send, ring_recv, prod, HALF, (0, 4, 8, 11))
    slot_step, slot_at, _ = ring(slot_out, slot_in, slot_send, slot_recv, slot_prod, SLOTS // 2, (0, 3, 6, 8))

    def end_copy(k, count, peer):
        where = pl.ds(k, count)
        return pltpu.make_async_remote_copy(
            end_out.at[where], end_in.at[where], end_send, end_recv, device_id={"tp": peer}, device_id_type=MESH
        )

    def slot_last(chain):
        same, away = own_side(slot_at(chain, len(blocks[chain]) - 1))
        end_out[2 * chain] = same.astype(BF16)
        end_out[2 * chain + 1] = away.astype(BF16)
        end_copy(2 * chain, 1, targets[chain]).start()
        end_copy(2 * chain + 1, 1, targets[chain] + 1 - 2 * x_hi).start()

    project(4)
    project(3)
    project(5)

    for chain in range(4):
        text_step(chain, 0)
    for o in (2, 6, 1, 7, 0):
        project(o)

    part_copy.wait_recv()
    image = (own_sum[...] + dot(slots_b, part_in[...]) + bias_ref[...]).astype(BF16)

    def exchange(out_ref, in_ref, send_sem, recv_sem):
        def start(i, _):
            peer = (lane + 1 + (i + 15) % 31) % LANES
            pltpu.make_async_remote_copy(
                out_ref.at[peer], in_ref.at[lane], send_sem, recv_sem, device_id={"lane": peer}, device_id_type=MESH
            ).start()
            return 0

        lax.fori_loop(0, LANES - 1, start, 0, unroll=True)
        in_ref[lane] = out_ref[lane]
        every = pl.ds(0, LANES - 1)
        whole = pltpu.make_async_remote_copy(
            out_ref.at[every],
            in_ref.at[every],
            send_sem,
            recv_sem,
            device_id={"lane": (lane + 1) % LANES},
            device_id_type=MESH,
        )
        return whole.wait_recv, whole.wait_send

    chunk_out[...] = to_chunks(image)
    lane_arrived, lane_sent = exchange(chunk_out, chunk_in, lane_send, lane_recv)

    load_kvg.wait()
    grad[...] = dot_t(kvg[...], kvw[...])

    for chain in range(4):
        text_step(chain, 1)
    for chain in range(4):
        if len(blocks[chain]) > 2:
            text_step(chain, 2)

    lane_arrived()
    arrived = from_chunks(chunk_in[...])
    slot_xg[...] = (arrived.astype(F32) * gain).astype(BF16)

    def slot_project(o):
        slot_prod[o] = dot(slot_xg[...], columns(o))

    slot_project(4)
    slot_step(0, 0)
    slot_step(1, 0)
    slot_project(3)
    slot_step(2, 0)
    slot_project(5)
    slot_step(3, 0)
    placed = dot(place.astype(BF16), arrived)
    wide = jnp.where(is_image, placed, text[...].astype(F32))
    stream[...] = wide
    squares = jnp.sum(wide * wide, axis=1, keepdims=True)
    dots = jnp.sum(wide * gain * grad[...], axis=1, keepdims=True)
    first = iota((TOKENS, 128), 1) == 0
    both = jnp.transpose(jnp.where(first, squares, dots))
    stat_out[...] = both[0:2, :]
    stat_in[tp] = both[0:2, :]

    def stat_start(i, _):
        pltpu.make_async_remote_copy(
            stat_out,
            stat_in.at[tp],
            stat_send,
            stat_recv,
            device_id={"tp": (tp + 1 + (i + 7) % 15) % TPS},
            device_id_type=MESH,
        ).start()
        return 0

    lax.fori_loop(0, TPS - 1, stat_start, 0, unroll=True)

    text_step(0, 3)
    text_step(1, 3)
    for o in (2, 6, 1, 7, 0):
        slot_project(o)
    for chain in range(4):
        slot_step(chain, 1)
    slot_kept, slot_away = own_side(slot_prod[0])
    end_out[8] = slot_away[0 : SLOTS // 2].astype(BF16)
    end_out[9] = slot_away[SLOTS // 2 :].astype(BF16)
    across = z * 2 + (1 - x_hi)
    end_copy(8, 2, across).start()

    text_first = prod[0, 0:HALF, :] + text_arrived(2, 2)
    text_last = prod[0, HALF:TOKENS, :] + text_arrived(3, 2)
    text_first = text_first + text_arrived(0, 3)
    text_last = text_last + text_arrived(1, 3)
    text_kept, text_away = own_side(jnp.concatenate([text_first, text_last], axis=0))
    cross_out[...] = text_away.astype(BF16)
    text_cross = pltpu.make_async_remote_copy(
        cross_out, cross_in, cross_send, cross_recv, device_id={"tp": across}, device_id_type=MESH
    )
    text_cross.start()

    each = pl.ds(0, TPS - 1)
    stat_whole = pltpu.make_async_remote_copy(
        stat_in.at[each], stat_in.at[each], stat_send, stat_recv, device_id={"tp": across}, device_id_type=MESH
    )
    stat_whole.wait_recv()
    totals = jnp.sum(stat_in[...], axis=0)
    inv_row = lax.rsqrt(totals[0:1, :] / D + EPSILON)
    inv = jnp.transpose(jnp.broadcast_to(inv_row, (128, TOKENS)))
    total_dots = jnp.transpose(jnp.broadcast_to(totals[1:2, :], (128, TOKENS)))
    factor = inv * inv * inv * total_dots / D
    inv4 = jnp.concatenate([inv] * 4, axis=1)
    factor4 = jnp.concatenate([factor] * 4, axis=1)
    embed = (inv4 * gain * grad[...] - stream[...] * factor4).astype(BF16)
    embed_out[...] = embed
    place_t = jnp.transpose(place).astype(BF16)
    back_out[...] = to_chunks(dot(place_t, embed).astype(BF16))
    back_arrived, back_sent = exchange(back_out, back_in, back_send, back_recv)

    slot_step(0, 2)
    slot_step(1, 2)
    slot_last(2)
    slot_last(3)
    slot_last(0)
    slot_last(1)

    back_arrived()
    returned = from_chunks(back_in[...])
    image_out[...] = dot(jnp.transpose(slots).astype(BF16), returned).astype(BF16)

    text_cross.wait_recv()
    text_sum = text_kept + cross_in[...].astype(F32)
    every_end = pltpu.make_async_remote_copy(
        end_out, end_in, end_send, end_recv, device_id={"tp": across}, device_id_type=MESH
    )
    every_end.wait_recv()

    def ends(up_or_down, own):
        total = None
        for k in up_or_down:
            part = end_in[k].astype(F32)
            total = part if total is None else total + part
        return total + own

    slot_sum = jnp.concatenate(
        [
            ends((0, 1, 4, 5, 8), slot_kept[0 : SLOTS // 2]),
            ends((2, 3, 6, 7, 9), slot_kept[SLOTS // 2 :]),
        ],
        axis=0,
    )
    high = slot_sum.astype(BF16)
    low = (slot_sum - high.astype(F32)).astype(BF16)
    place_b = place.astype(BF16)
    slot_placed = dot(place_b, high) + dot(place_b, low)
    kv_out[...] = (inv * jnp.where(is_image, slot_placed, text_sum)).astype(BF16)

    part_copy.wait_send()
    lane_sent()
    back_sent()
    stat_whole.wait_send()
    for out_ref, sem, count in ((ring_out, ring_send, 14), (slot_out, slot_send, 10)):
        sent = out_ref.at[pl.ds(0, count)]
        pltpu.make_async_remote_copy(
            sent, sent, sem, sem, device_id={"tp": across}, device_id_type=MESH
        ).wait_send()
    every_end.wait_send()
    text_cross.wait_send()


def finish(kv, embed, image, kv_hbm, embed_hbm, image_hbm, sems):
    copies = []
    for k, (src, dst) in enumerate(((embed, embed_hbm), (image, image_hbm), (kv, kv_hbm))):
        copy = pltpu.make_async_copy(src, dst, sems.at[k])
        copy.start()
        copies.append(copy)
    for copy in copies:
        copy.wait()


def on_device(
    merge_hidden,
    merge_weight,
    merge_bias,
    row_dest,
    image_pos,
    text_embed,
    norm_gain,
    kv_weight,
    kv_grad,
):
    any_space = pl.BlockSpec(memory_space=pl.ANY)
    vmem = pl.BlockSpec(memory_space=pltpu.VMEM)
    dma = pltpu.SemaphoreType.DMA
    shapes = ((TOKENS, KV2 // TPS), (TOKENS, WIDTH), (ROWS, WIDTH))
    results = pl.pallas_call(
        kernel,
        name="step",
        out_shape=tuple(pltpu.VMEM(shape, BF16) for shape in shapes),
        in_specs=[any_space] * 9,
        out_specs=(vmem, vmem, vmem),
        scratch_shapes=[
            pltpu.VMEM((2, ROWS, VD_DEV), BF16),
            pltpu.VMEM((VD_DEV, WIDTH), BF16),
            pltpu.VMEM((1, WIDTH), F32),
            pltpu.VMEM((1, ROWS), jnp.int32),
            pltpu.VMEM((CAP, LANES), jnp.int32),
            pltpu.VMEM((TOKENS, WIDTH), BF16),
            pltpu.VMEM((1, WIDTH), F32),
            pltpu.VMEM((WIDTH, KV2), BF16),
            pltpu.VMEM((TOKENS, KV2), BF16),
            pltpu.VMEM((SLOTS, WIDTH), F32),
            pltpu.VMEM((ROWS, WIDTH), BF16),
            pltpu.VMEM((ROWS, WIDTH), BF16),
            pltpu.VMEM((TOKENS, WIDTH), F32),
            pltpu.VMEM((TOKENS, WIDTH), F32),
            pltpu.VMEM((LANES, 16, 128), BF16),
            pltpu.VMEM((LANES, 16, 128), BF16),
            pltpu.VMEM((LANES, 16, 128), BF16),
            pltpu.VMEM((LANES, 16, 128), BF16),
            pltpu.VMEM((2, TOKENS), F32),
            pltpu.VMEM((TPS, 2, TOKENS), F32),
            pltpu.VMEM((TOKENS, WIDTH), BF16),
            pltpu.VMEM((ZS, TOKENS, 256), F32),
            pltpu.VMEM((14, HALF, 256), BF16),
            pltpu.VMEM((14, HALF, 256), BF16),
            pltpu.VMEM((SLOTS, WIDTH), BF16),
            pltpu.VMEM((ZS, SLOTS, 256), F32),
            pltpu.VMEM((10, SLOTS // 2, 256), BF16),
            pltpu.VMEM((10, SLOTS // 2, 256), BF16),
            pltpu.VMEM((TOKENS, 128), BF16),
            pltpu.VMEM((TOKENS, 128), BF16),
            pltpu.VMEM((10, SLOTS // 2, 128), BF16),
            pltpu.VMEM((10, SLOTS // 2, 128), BF16),
            dma((10,)),
            pltpu.SemaphoreType.DMA,
            pltpu.SemaphoreType.DMA,
            pltpu.SemaphoreType.DMA,
            pltpu.SemaphoreType.DMA,
            pltpu.SemaphoreType.DMA,
            pltpu.SemaphoreType.DMA,
            pltpu.SemaphoreType.DMA,
            pltpu.SemaphoreType.DMA,
            pltpu.SemaphoreType.DMA,
            dma((14,)),
            pltpu.SemaphoreType.DMA,
            dma((10,)),
            pltpu.SemaphoreType.DMA,
            pltpu.SemaphoreType.DMA,
            pltpu.SemaphoreType.DMA,
            pltpu.SemaphoreType.DMA,
        ],
        compiler_params=pltpu.CompilerParams(
            collective_id=0, has_side_effects=True, vmem_limit_bytes=65011712
        ),
    )(
        merge_hidden,
        merge_weight,
        merge_bias.reshape(1, WIDTH),
        row_dest.reshape(1, ROWS),
        jnp.transpose(image_pos.reshape(LANES, CAP)),
        text_embed,
        norm_gain.reshape(1, WIDTH),
        kv_weight,
        kv_grad,
    )
    return pl.pallas_call(
        finish,
        name="finish",
        out_shape=tuple(jax.ShapeDtypeStruct(shape, BF16) for shape in shapes),
        in_specs=[vmem] * 3,
        out_specs=(any_space,) * 3,
        scratch_shapes=[dma((3,))],
        compiler_params=pltpu.CompilerParams(vmem_limit_bytes=4 * 1024 * 1024),
    )(*results)


def solution(mesh):
    in_specs = (
        P("lane", "section"),
        P("section", "tp"),
        P("tp"),
        P(("lane", "section")),
        P("lane", "section", None, None),
        P(("lane", "section"), "tp"),
        P("tp"),
        P("tp", None),
        P(("lane", "section"), None),
    )
    out_specs = (
        P(("lane", "section"), "tp"),
        P(("lane", "section"), "tp"),
        P(("lane", "section"), "tp"),
    )
    return jax.shard_map(on_device, mesh=mesh, in_specs=in_specs, out_specs=out_specs, check_vma=False)
```

```python
import functools

import jax
import jax.numpy as jnp
from jax import lax
from jax.experimental import pallas as pl
from jax.experimental.pallas import tpu as pltpu
from jax.sharding import PartitionSpec as P

MESH = pl.DeviceIdType.MESH
D = 8192
EPSILON = 1e-06
LANES = 32
TPS = 16
ZS = 8
CAP = 4
SLOTS = LANES * CAP
ROWS = 256
TOKENS = 256
WIDTH = 512
HALF = TOKENS // 2
KV2 = 2048
VD_DEV = 2560
CHUNK = 512
BF16 = jnp.bfloat16
F32 = jnp.float32


def erf(x):
    x = jnp.clip(x, -3.832506856900711, 3.832506856900711)
    y = x * x
    top = 0.00022905065861350646
    for c in (0.0034082910107109506, 0.050955695062380861, 0.18520832239976145, 1.128379143519084):
        top = top * y + c
    low = -1.1791602954361697e-7
    for c in (
        0.000023547966471313185,
        0.0010179625278914885,
        0.014070470171167667,
        0.11098505178285362,
        0.49746925110067538,
        1.0,
    ):
        low = low * y + c
    return x * top / low


def gelu(x):
    return 0.5 * x * (1.0 + erf(x * 0.7071067811865476))


def iota(shape, dim):
    return lax.broadcasted_iota(jnp.int32, shape, dim)


def dot(a, b):
    return jnp.dot(a, b, preferred_element_type=F32)


def dot_t(a, b):
    return lax.dot_general(a, b, (((1,), (1,)), ((), ())), preferred_element_type=F32)


def send_slots(dest):
    lanes = iota((LANES, ROWS), 0)
    matches = lanes == dest
    ones = matches.astype(F32)
    earlier = (iota((ROWS, ROWS), 0) < iota((ROWS, ROWS), 1)).astype(F32)
    before = dot(ones.astype(BF16), earlier.astype(BF16))
    rank = jnp.sum(before * ones, axis=0, keepdims=True).astype(jnp.int32)
    slot = jnp.where(dest >= 0, dest * CAP + rank, -1)
    return (iota((SLOTS, ROWS), 0) == slot).astype(F32)


def to_chunks(rows):
    total = None
    i = iota((SLOTS * 4, SLOTS), 0)
    j = iota((SLOTS * 4, SLOTS), 1)
    for c in range(4):
        pick = (i == (j // 4) * 16 + c * 4 + j % 4).astype(F32).astype(BF16)
        part = dot(pick, rows[:, c * 128 : (c + 1) * 128])
        total = part if total is None else total + part
    return total.astype(BF16).reshape(LANES, 16, 128)


def from_chunks(chunks):
    i = iota((SLOTS, SLOTS * 4), 1)
    j = iota((SLOTS, SLOTS * 4), 0)
    flat = chunks.reshape(SLOTS * 4, 128)
    parts = []
    for c in range(4):
        pick = (i == (j // 4) * 16 + c * 4 + j % 4).astype(F32).astype(BF16)
        parts.append(dot(pick, flat))
    return jnp.concatenate(parts, axis=1).astype(BF16)


def kernel(
    hidden_hbm,
    weight_hbm,
    bias_hbm,
    dest_hbm,
    pos_hbm,
    text_hbm,
    gain_hbm,
    kvw_hbm,
    kvg_hbm,
    kv_out,
    embed_out,
    image_out,
    hidden,
    weight,
    bias_ref,
    dest_ref,
    pos_ref,
    text,
    gain_ref,
    kvw,
    kvg,
    own_sum,
    part_out,
    part_in,
    grad,
    stream,
    chunk_out,
    chunk_in,
    image_rows,
    grad_rows,
    back_out,
    back_in,
    stat_out,
    stat_in,
    xg,
    prod,
    ring_out,
    ring_in,
    slot_xg,
    slot_prod,
    slot_out,
    slot_in,
    cross_out,
    cross_in,
    end_out,
    end_in,
    load_sem,
    sec_send,
    sec_recv,
    lane_send,
    lane_recv,
    back_send,
    back_recv,
    stat_send,
    stat_recv,
    ring_send,
    ring_recv,
    slot_send,
    slot_recv,
    end_send,
    end_recv,
    cross_send,
    cross_recv,
):
    lane = lax.axis_index("lane")
    section = lax.axis_index("section")
    tp = lax.axis_index("tp")
    z = tp // 2
    x_hi = tp % 2
    other = 1 - section

    barrier = pltpu.get_barrier_semaphore()

    def greet_lane(i, _):
        p = 1 + (i + 15) % 31
        pl.semaphore_signal(barrier, inc=1, device_id={"lane": (lane + p) % LANES}, device_id_type=MESH)
        return 0

    def greet_tp(i, _):
        p = 1 + (i + 7) % 15
        pl.semaphore_signal(barrier, inc=1, device_id={"tp": (tp + p) % TPS}, device_id_type=MESH)
        return 0

    def load(src, dst, k):
        copy = pltpu.make_async_copy(src, dst, load_sem.at[k])
        copy.start()
        return copy

    load_dest = load(dest_hbm, dest_ref, 0)
    load_own = load(hidden_hbm.at[pl.ds(section * ROWS, ROWS)], hidden.at[0], 1)
    load_weight = load(weight_hbm, weight, 2)
    lax.fori_loop(0, LANES - 1, greet_lane, 0, unroll=True)
    lax.fori_loop(0, TPS - 1, greet_tp, 0, unroll=True)
    pl.semaphore_signal(barrier, inc=1, device_id={"section": other}, device_id_type=MESH)
    load_dest.wait()
    slots = send_slots(dest_ref[...])
    slots_b = slots.astype(BF16)
    load_own.wait()
    load_weight.wait()
    load_other = load(hidden_hbm.at[pl.ds(other * ROWS, ROWS)], hidden.at[1], 3)
    load_pos = load(pos_hbm, pos_ref, 4)
    load_gain = load(gain_hbm, gain_ref, 5)
    load_bias = load(bias_hbm, bias_ref, 6)
    load_text = load(text_hbm, text, 7)
    load_kvw = load(kvw_hbm, kvw, 8)
    load_kvg = load(kvg_hbm, kvg, 9)
    total = None
    for k in range(VD_DEV // CHUNK):
        cols = slice(k * CHUNK, (k + 1) * CHUNK)
        picked = dot(slots_b, hidden[0, :, cols])
        part = dot(gelu(picked).astype(BF16), weight[cols, :])
        total = part if total is None else total + part
    own_sum[...] = total

    load_other.wait()
    for half in range(2):
        rows = slice(half * HALF, (half + 1) * HALF)
        total = None
        for k in range(VD_DEV // CHUNK):
            cols = slice(k * CHUNK, (k + 1) * CHUNK)
            wide = hidden[1, rows, cols].astype(F32)
            part = dot(gelu(wide).astype(BF16), weight[cols, :])
            total = part if total is None else total + part
        part_out[rows, :] = total.astype(BF16)

    pl.semaphore_wait(barrier, 1 + (LANES - 1) + (TPS - 1))
    part_copy = pltpu.make_async_remote_copy(
        part_out, part_in, sec_send, sec_recv, device_id={"section": other}, device_id_type=MESH
    )
    part_copy.start()
    load_pos.wait()
    spread = (iota((LANES, SLOTS), 1) // CAP == iota((LANES, SLOTS), 0)).astype(F32)
    pos_all = dot(pos_ref[...].astype(F32).astype(BF16), spread.astype(BF16))
    pos_own = iota((CAP, SLOTS), 1) % CAP == iota((CAP, SLOTS), 0)
    pos = jnp.sum(jnp.where(pos_own, pos_all, 0.0), axis=0, keepdims=True)
    place = (iota((TOKENS, SLOTS), 0) == pos.astype(jnp.int32)).astype(F32)
    is_image = jnp.sum(place, axis=1, keepdims=True) > 0.5

    load_gain.wait()
    load_bias.wait()
    load_text.wait()
    load_kvw.wait()
    gain = gain_ref[...]
    xg[...] = jnp.where(is_image, 0.0, text[...].astype(F32) * gain).astype(BF16)

    def columns(o):
        block = (z + o) % ZS
        return kvw[:, pl.ds(pl.multiple_of(block * 256, 256), 256)]

    def project(o):
        prod[o] = dot(xg[...], columns(o))

    up = ((z + 1) % ZS) * 2 + x_hi
    down = ((z + ZS - 1) % ZS) * 2 + x_hi
    blocks = ((4, 5, 6, 7), (4, 3, 2, 1), (3, 2, 1), (5, 6, 7))
    targets = (down, up, up, down)
    firsts = (True, False, True, False)

    def ring(out_ref, in_ref, send_sem, recv_sem, prod_ref, half, offsets):
        def copy_of(chain, step):
            k = offsets[chain] + step
            return pltpu.make_async_remote_copy(
                out_ref.at[k],
                in_ref.at[k],
                send_sem,
                recv_sem.at[k],
                device_id={"tp": targets[chain]},
                device_id_type=MESH,
            )

        def sum_at(chain, step):
            rows = slice(0, half) if firsts[chain] else slice(half, 2 * half)
            own = prod_ref[blocks[chain][step], rows, :]
            if step > 0:
                copy_of(chain, step - 1).wait_recv()
                own = own + in_ref[offsets[chain] + step - 1].astype(F32)
            return own

        def step_of(chain, step):
            out_ref[offsets[chain] + step] = sum_at(chain, step).astype(BF16)
            copy_of(chain, step).start()

        def arrived_at(chain, step):
            copy_of(chain, step).wait_recv()
            return in_ref[offsets[chain] + step].astype(F32)

        return step_of, sum_at, arrived_at

    def own_side(block):
        left, right = block[:, 0:128], block[:, 128:256]
        return jnp.where(x_hi == 0, left, right), jnp.where(x_hi == 0, right, left)

    text_step, _, text_arrived = ring(ring_out, ring_in, ring_send, ring_recv, prod, HALF, (0, 4, 8, 11))
    slot_step, slot_at, _ = ring(slot_out, slot_in, slot_send, slot_recv, slot_prod, SLOTS // 2, (0, 3, 6, 8))

    def end_copy(k, count, peer):
        where = pl.ds(k, count)
        return pltpu.make_async_remote_copy(
            end_out.at[where], end_in.at[where], end_send, end_recv, device_id={"tp": peer}, device_id_type=MESH
        )

    def slot_last(chain):
        same, away = own_side(slot_at(chain, len(blocks[chain]) - 1))
        end_out[2 * chain] = same.astype(BF16)
        end_out[2 * chain + 1] = away.astype(BF16)
        end_copy(2 * chain, 1, targets[chain]).start()
        end_copy(2 * chain + 1, 1, targets[chain] + 1 - 2 * x_hi).start()

    project(4)
    project(3)
    project(5)

    for chain in range(4):
        text_step(chain, 0)
    for o in (2, 6, 1, 7, 0):
        project(o)

    part_copy.wait_recv()
    image = (own_sum[...] + dot(slots_b, part_in[...]) + bias_ref[...]).astype(BF16)
    image_rows[...] = image

    def exchange(out_ref, in_ref, send_sem, recv_sem):
        def start(i, _):
            peer = (lane + 1 + (i + 15) % 31) % LANES
            pltpu.make_async_remote_copy(
                out_ref.at[peer], in_ref.at[lane], send_sem, recv_sem, device_id={"lane": peer}, device_id_type=MESH
            ).start()
            return 0

        lax.fori_loop(0, LANES - 1, start, 0, unroll=True)
        in_ref[lane] = out_ref[lane]
        every = pl.ds(0, LANES - 1)
        whole = pltpu.make_async_remote_copy(
            out_ref.at[every],
            in_ref.at[every],
            send_sem,
            recv_sem,
            device_id={"lane": (lane + 1) % LANES},
            device_id_type=MESH,
        )
        return whole.wait_recv, whole.wait_send

    chunk_out[...] = to_chunks(image)
    lane_arrived, lane_sent = exchange(chunk_out, chunk_in, lane_send, lane_recv)

    load_kvg.wait()
    normed_grad = dot_t(kvg[...], kvw[...])
    grad[...] = normed_grad
    place_t = jnp.transpose(place).astype(BF16)
    back_out[...] = to_chunks(dot(place_t, normed_grad.astype(BF16)).astype(BF16))
    back_arrived, back_sent = exchange(back_out, back_in, back_send, back_recv)

    for chain in range(4):
        text_step(chain, 1)
    for chain in range(4):
        if len(blocks[chain]) > 2:
            text_step(chain, 2)

    lane_arrived()
    arrived = from_chunks(chunk_in[...])
    slot_xg[...] = (arrived.astype(F32) * gain).astype(BF16)

    def slot_project(o):
        slot_prod[o] = dot(slot_xg[...], columns(o))

    slot_project(4)
    slot_step(0, 0)
    slot_step(1, 0)
    slot_project(3)
    slot_step(2, 0)
    slot_project(5)
    slot_step(3, 0)
    text_step(0, 3)
    text_step(1, 3)
    for o in (2, 6, 1, 7, 0):
        slot_project(o)
    placed = dot(place.astype(BF16), arrived)
    wide = jnp.where(is_image, placed, text[...].astype(F32))
    stream[...] = wide
    squares = jnp.sum(wide * wide, axis=1, keepdims=True)
    dots = jnp.sum(wide * gain * grad[...], axis=1, keepdims=True)
    first = iota((TOKENS, 128), 1) == 0
    both = jnp.transpose(jnp.where(first, squares, dots))
    stat_out[:, 0:TOKENS] = both[0:2, :]

    back_arrived()
    grad_rows[...] = from_chunks(back_in[...])
    rows_wide = image_rows[...].astype(F32)
    row_squares = jnp.sum(rows_wide * rows_wide, axis=1, keepdims=True)
    row_dots = jnp.sum(rows_wide * gain * grad_rows[...].astype(F32), axis=1, keepdims=True)
    row_both = jnp.transpose(jnp.where(iota((SLOTS, 128), 1) == 0, row_squares, row_dots))
    stat_out[:, TOKENS:] = row_both[0:2, :]
    stat_in[tp] = stat_out[...]

    def stat_start(i, _):
        pltpu.make_async_remote_copy(
            stat_out,
            stat_in.at[tp],
            stat_send,
            stat_recv,
            device_id={"tp": (tp + 1 + (i + 7) % 15) % TPS},
            device_id_type=MESH,
        ).start()
        return 0

    lax.fori_loop(0, TPS - 1, stat_start, 0, unroll=True)

    for chain in range(4):
        slot_step(chain, 1)
    slot_kept, slot_away = own_side(slot_prod[0])
    end_out[8] = slot_away[0 : SLOTS // 2].astype(BF16)
    end_out[9] = slot_away[SLOTS // 2 :].astype(BF16)
    across = z * 2 + (1 - x_hi)
    end_copy(8, 2, across).start()

    text_first = prod[0, 0:HALF, :] + text_arrived(2, 2)
    text_last = prod[0, HALF:TOKENS, :] + text_arrived(3, 2)
    text_first = text_first + text_arrived(0, 3)
    text_last = text_last + text_arrived(1, 3)
    text_kept, text_away = own_side(jnp.concatenate([text_first, text_last], axis=0))
    cross_out[...] = text_away.astype(BF16)
    text_cross = pltpu.make_async_remote_copy(
        cross_out, cross_in, cross_send, cross_recv, device_id={"tp": across}, device_id_type=MESH
    )
    text_cross.start()

    slot_step(0, 2)
    slot_step(1, 2)
    slot_last(2)
    slot_last(3)
    slot_last(0)
    slot_last(1)

    each = pl.ds(0, TPS - 1)
    stat_whole = pltpu.make_async_remote_copy(
        stat_in.at[each], stat_in.at[each], stat_send, stat_recv, device_id={"tp": across}, device_id_type=MESH
    )
    stat_whole.wait_recv()
    totals = jnp.sum(stat_in[...], axis=0)
    inv_row = lax.rsqrt(totals[0:1, :] / D + EPSILON)

    def gradient(where, count, wide, grads):
        inv = jnp.transpose(jnp.broadcast_to(inv_row[:, where], (128, count)))
        total_dots = jnp.transpose(jnp.broadcast_to(totals[1:2, where], (128, count)))
        factor = inv * inv * inv * total_dots / D
        inv4 = jnp.concatenate([inv] * 4, axis=1)
        factor4 = jnp.concatenate([factor] * 4, axis=1)
        return inv, (inv4 * gain * grads - wide * factor4).astype(BF16)

    inv, embed_out[...] = gradient(slice(0, TOKENS), TOKENS, stream[...], grad[...])
    _, row_grad = gradient(
        slice(TOKENS, TOKENS + SLOTS), SLOTS, image_rows[...].astype(F32), grad_rows[...].astype(F32)
    )
    image_out[...] = dot(jnp.transpose(slots).astype(BF16), row_grad).astype(BF16)

    text_cross.wait_recv()
    text_sum = text_kept + cross_in[...].astype(F32)
    every_end = pltpu.make_async_remote_copy(
        end_out, end_in, end_send, end_recv, device_id={"tp": across}, device_id_type=MESH
    )
    every_end.wait_recv()

    def ends(up_or_down, own):
        total = None
        for k in up_or_down:
            part = end_in[k].astype(F32)
            total = part if total is None else total + part
        return total + own

    slot_sum = jnp.concatenate(
        [
            ends((0, 1, 4, 5, 8), slot_kept[0 : SLOTS // 2]),
            ends((2, 3, 6, 7, 9), slot_kept[SLOTS // 2 :]),
        ],
        axis=0,
    )
    high = slot_sum.astype(BF16)
    low = (slot_sum - high.astype(F32)).astype(BF16)
    place_b = place.astype(BF16)
    slot_placed = dot(place_b, high) + dot(place_b, low)
    kv_out[...] = (inv * jnp.where(is_image, slot_placed, text_sum)).astype(BF16)

    part_copy.wait_send()
    lane_sent()
    back_sent()
    stat_whole.wait_send()
    for out_ref, sem, count in ((ring_out, ring_send, 14), (slot_out, slot_send, 10)):
        sent = out_ref.at[pl.ds(0, count)]
        pltpu.make_async_remote_copy(
            sent, sent, sem, sem, device_id={"tp": across}, device_id_type=MESH
        ).wait_send()
    every_end.wait_send()
    text_cross.wait_send()


def finish(kv, embed, image, kv_hbm, embed_hbm, image_hbm, sems):
    copies = []
    for k, (src, dst) in enumerate(((embed, embed_hbm), (image, image_hbm), (kv, kv_hbm))):
        copy = pltpu.make_async_copy(src, dst, sems.at[k])
        copy.start()
        copies.append(copy)
    for copy in copies:
        copy.wait()


def on_device(
    merge_hidden,
    merge_weight,
    merge_bias,
    row_dest,
    image_pos,
    text_embed,
    norm_gain,
    kv_weight,
    kv_grad,
):
    any_space = pl.BlockSpec(memory_space=pl.ANY)
    vmem = pl.BlockSpec(memory_space=pltpu.VMEM)
    dma = pltpu.SemaphoreType.DMA
    shapes = ((TOKENS, KV2 // TPS), (TOKENS, WIDTH), (ROWS, WIDTH))
    results = pl.pallas_call(
        kernel,
        name="step",
        out_shape=tuple(pltpu.VMEM(shape, BF16) for shape in shapes),
        in_specs=[any_space] * 9,
        out_specs=(vmem, vmem, vmem),
        scratch_shapes=[
            pltpu.VMEM((2, ROWS, VD_DEV), BF16),
            pltpu.VMEM((VD_DEV, WIDTH), BF16),
            pltpu.VMEM((1, WIDTH), F32),
            pltpu.VMEM((1, ROWS), jnp.int32),
            pltpu.VMEM((CAP, LANES), jnp.int32),
            pltpu.VMEM((TOKENS, WIDTH), BF16),
            pltpu.VMEM((1, WIDTH), F32),
            pltpu.VMEM((WIDTH, KV2), BF16),
            pltpu.VMEM((TOKENS, KV2), BF16),
            pltpu.VMEM((SLOTS, WIDTH), F32),
            pltpu.VMEM((ROWS, WIDTH), BF16),
            pltpu.VMEM((ROWS, WIDTH), BF16),
            pltpu.VMEM((TOKENS, WIDTH), F32),
            pltpu.VMEM((TOKENS, WIDTH), F32),
            pltpu.VMEM((LANES, 16, 128), BF16),
            pltpu.VMEM((LANES, 16, 128), BF16),
            pltpu.VMEM((SLOTS, WIDTH), BF16),
            pltpu.VMEM((SLOTS, WIDTH), BF16),
            pltpu.VMEM((LANES, 16, 128), BF16),
            pltpu.VMEM((LANES, 16, 128), BF16),
            pltpu.VMEM((2, TOKENS + SLOTS), F32),
            pltpu.VMEM((TPS, 2, TOKENS + SLOTS), F32),
            pltpu.VMEM((TOKENS, WIDTH), BF16),
            pltpu.VMEM((ZS, TOKENS, 256), F32),
            pltpu.VMEM((14, HALF, 256), BF16),
            pltpu.VMEM((14, HALF, 256), BF16),
            pltpu.VMEM((SLOTS, WIDTH), BF16),
            pltpu.VMEM((ZS, SLOTS, 256), F32),
            pltpu.VMEM((10, SLOTS // 2, 256), BF16),
            pltpu.VMEM((10, SLOTS // 2, 256), BF16),
            pltpu.VMEM((TOKENS, 128), BF16),
            pltpu.VMEM((TOKENS, 128), BF16),
            pltpu.VMEM((10, SLOTS // 2, 128), BF16),
            pltpu.VMEM((10, SLOTS // 2, 128), BF16),
            dma((10,)),
            pltpu.SemaphoreType.DMA,
            pltpu.SemaphoreType.DMA,
            pltpu.SemaphoreType.DMA,
            pltpu.SemaphoreType.DMA,
            pltpu.SemaphoreType.DMA,
            pltpu.SemaphoreType.DMA,
            pltpu.SemaphoreType.DMA,
            pltpu.SemaphoreType.DMA,
            pltpu.SemaphoreType.DMA,
            dma((14,)),
            pltpu.SemaphoreType.DMA,
            dma((10,)),
            pltpu.SemaphoreType.DMA,
            pltpu.SemaphoreType.DMA,
            pltpu.SemaphoreType.DMA,
            pltpu.SemaphoreType.DMA,
        ],
        compiler_params=pltpu.CompilerParams(
            collective_id=0, has_side_effects=True, vmem_limit_bytes=65011712
        ),
    )(
        merge_hidden,
        merge_weight,
        merge_bias.reshape(1, WIDTH),
        row_dest.reshape(1, ROWS),
        jnp.transpose(image_pos.reshape(LANES, CAP)),
        text_embed,
        norm_gain.reshape(1, WIDTH),
        kv_weight,
        kv_grad,
    )
    return pl.pallas_call(
        finish,
        name="finish",
        out_shape=tuple(jax.ShapeDtypeStruct(shape, BF16) for shape in shapes),
        in_specs=[vmem] * 3,
        out_specs=(any_space,) * 3,
        scratch_shapes=[dma((3,))],
        compiler_params=pltpu.CompilerParams(vmem_limit_bytes=4 * 1024 * 1024),
    )(*results)


def solution(mesh):
    in_specs = (
        P("lane", "section"),
        P("section", "tp"),
        P("tp"),
        P(("lane", "section")),
        P("lane", "section", None, None),
        P(("lane", "section"), "tp"),
        P("tp"),
        P("tp", None),
        P(("lane", "section"), None),
    )
    out_specs = (
        P(("lane", "section"), "tp"),
        P(("lane", "section"), "tp"),
        P(("lane", "section"), "tp"),
    )
    return jax.shard_map(on_device, mesh=mesh, in_specs=in_specs, out_specs=out_specs, check_vma=False)
```

```python
import functools

import jax
import jax.numpy as jnp
from jax import lax
from jax.experimental import pallas as pl
from jax.experimental.pallas import tpu as pltpu
from jax.sharding import PartitionSpec as P

MESH = pl.DeviceIdType.MESH
D = 8192
EPSILON = 1e-06
LANES = 32
TPS = 16
ZS = 8
CAP = 4
SLOTS = LANES * CAP
ROWS = 256
TOKENS = 256
WIDTH = 512
HALF = TOKENS // 2
KV2 = 2048
VD_DEV = 2560
CHUNK = 512
BF16 = jnp.bfloat16
F32 = jnp.float32


def erf(x):
    x = jnp.clip(x, -3.832506856900711, 3.832506856900711)
    y = x * x
    top = 0.00022905065861350646
    for c in (0.0034082910107109506, 0.050955695062380861, 0.18520832239976145, 1.128379143519084):
        top = top * y + c
    low = -1.1791602954361697e-7
    for c in (
        0.000023547966471313185,
        0.0010179625278914885,
        0.014070470171167667,
        0.11098505178285362,
        0.49746925110067538,
        1.0,
    ):
        low = low * y + c
    return x * top / low


def gelu(x):
    return 0.5 * x * (1.0 + erf(x * 0.7071067811865476))


def iota(shape, dim):
    return lax.broadcasted_iota(jnp.int32, shape, dim)


def dot(a, b):
    return jnp.dot(a, b, preferred_element_type=F32)


def dot_t(a, b):
    return lax.dot_general(a, b, (((1,), (1,)), ((), ())), preferred_element_type=F32)


def send_slots(dest):
    lanes = iota((LANES, ROWS), 0)
    matches = lanes == dest
    ones = matches.astype(F32)
    earlier = (iota((ROWS, ROWS), 0) < iota((ROWS, ROWS), 1)).astype(F32)
    before = dot(ones.astype(BF16), earlier.astype(BF16))
    rank = jnp.sum(before * ones, axis=0, keepdims=True).astype(jnp.int32)
    slot = jnp.where(dest >= 0, dest * CAP + rank, -1)
    return (iota((SLOTS, ROWS), 0) == slot).astype(F32)


def to_chunks(rows):
    total = None
    i = iota((SLOTS * 4, SLOTS), 0)
    j = iota((SLOTS * 4, SLOTS), 1)
    for c in range(4):
        pick = (i == (j // 4) * 16 + c * 4 + j % 4).astype(F32).astype(BF16)
        part = dot(pick, rows[:, c * 128 : (c + 1) * 128])
        total = part if total is None else total + part
    return total.astype(BF16).reshape(LANES, 16, 128)


def from_chunks(chunks):
    i = iota((SLOTS, SLOTS * 4), 1)
    j = iota((SLOTS, SLOTS * 4), 0)
    flat = chunks.reshape(SLOTS * 4, 128)
    parts = []
    for c in range(4):
        pick = (i == (j // 4) * 16 + c * 4 + j % 4).astype(F32).astype(BF16)
        parts.append(dot(pick, flat))
    return jnp.concatenate(parts, axis=1).astype(BF16)


def kernel(
    hidden_hbm,
    weight_hbm,
    bias_hbm,
    dest_hbm,
    pos_hbm,
    text_hbm,
    gain_hbm,
    kvw_hbm,
    kvg_hbm,
    kv_out,
    embed_out,
    image_out,
    hidden,
    weight,
    bias_ref,
    dest_ref,
    pos_ref,
    text,
    gain_ref,
    kvw,
    kvg,
    own_sum,
    part_out,
    part_in,
    grad,
    stream,
    chunk_out,
    chunk_in,
    image_rows,
    grad_rows,
    back_out,
    back_in,
    stat_out,
    stat_in,
    xg,
    prod,
    ring_out,
    ring_in,
    slot_xg,
    slot_prod,
    slot_out,
    slot_in,
    cross_out,
    cross_in,
    end_out,
    end_in,
    load_sem,
    sec_send,
    sec_recv,
    lane_send,
    lane_recv,
    back_send,
    back_recv,
    stat_send,
    stat_recv,
    ring_send,
    ring_recv,
    slot_send,
    slot_recv,
    end_send,
    end_recv,
    cross_send,
    cross_recv,
):
    lane = lax.axis_index("lane")
    section = lax.axis_index("section")
    tp = lax.axis_index("tp")
    z = tp // 2
    x_hi = tp % 2
    other = 1 - section

    barrier = pltpu.get_barrier_semaphore()

    def greet_lane(i, _):
        p = 1 + (i + 15) % 31
        pl.semaphore_signal(barrier, inc=1, device_id={"lane": (lane + p) % LANES}, device_id_type=MESH)
        return 0

    def greet_tp(i, _):
        p = 1 + (i + 7) % 15
        pl.semaphore_signal(barrier, inc=1, device_id={"tp": (tp + p) % TPS}, device_id_type=MESH)
        return 0

    def load(src, dst, k):
        copy = pltpu.make_async_copy(src, dst, load_sem.at[k])
        copy.start()
        return copy

    load_dest = load(dest_hbm, dest_ref, 0)
    load_own = load(hidden_hbm.at[pl.ds(section * ROWS, ROWS)], hidden.at[0], 1)
    load_weight = load(weight_hbm, weight, 2)
    lax.fori_loop(0, LANES - 1, greet_lane, 0, unroll=True)
    lax.fori_loop(0, TPS - 1, greet_tp, 0, unroll=True)
    pl.semaphore_signal(barrier, inc=1, device_id={"section": other}, device_id_type=MESH)
    load_dest.wait()
    slots = send_slots(dest_ref[...])
    slots_b = slots.astype(BF16)
    load_own.wait()
    load_weight.wait()
    load_other = load(hidden_hbm.at[pl.ds(other * ROWS, ROWS)], hidden.at[1], 3)
    load_pos = load(pos_hbm, pos_ref, 4)
    load_gain = load(gain_hbm, gain_ref, 5)
    load_bias = load(bias_hbm, bias_ref, 6)
    load_text = load(text_hbm, text, 7)
    load_kvw = load(kvw_hbm, kvw, 8)
    load_kvg = load(kvg_hbm, kvg, 9)
    total = None
    for k in range(VD_DEV // CHUNK):
        cols = slice(k * CHUNK, (k + 1) * CHUNK)
        picked = dot(slots_b, hidden[0, :, cols])
        part = dot(gelu(picked).astype(BF16), weight[cols, :])
        total = part if total is None else total + part
    own_sum[...] = total

    load_other.wait()
    for half in range(2):
        rows = slice(half * HALF, (half + 1) * HALF)
        total = None
        for k in range(VD_DEV // CHUNK):
            cols = slice(k * CHUNK, (k + 1) * CHUNK)
            wide = hidden[1, rows, cols].astype(F32)
            part = dot(gelu(wide).astype(BF16), weight[cols, :])
            total = part if total is None else total + part
        part_out[rows, :] = total.astype(BF16)

    pl.semaphore_wait(barrier, 1 + (LANES - 1) + (TPS - 1))
    part_copy = pltpu.make_async_remote_copy(
        part_out, part_in, sec_send, sec_recv, device_id={"section": other}, device_id_type=MESH
    )
    part_copy.start()
    load_pos.wait()
    spread = (iota((LANES, SLOTS), 1) // CAP == iota((LANES, SLOTS), 0)).astype(F32)
    pos_all = dot(pos_ref[...].astype(F32).astype(BF16), spread.astype(BF16))
    pos_own = iota((CAP, SLOTS), 1) % CAP == iota((CAP, SLOTS), 0)
    pos = jnp.sum(jnp.where(pos_own, pos_all, 0.0), axis=0, keepdims=True)
    place = (iota((TOKENS, SLOTS), 0) == pos.astype(jnp.int32)).astype(F32)
    is_image = jnp.sum(place, axis=1, keepdims=True) > 0.5

    load_gain.wait()
    load_bias.wait()
    load_text.wait()
    load_kvw.wait()
    gain = gain_ref[...]
    xg[...] = jnp.where(is_image, 0.0, text[...].astype(F32) * gain).astype(BF16)

    def columns(o):
        block = (z + o) % ZS
        return kvw[:, pl.ds(pl.multiple_of(block * 256, 256), 256)]

    def project(o):
        prod[o] = dot(xg[...], columns(o))

    up = ((z + 1) % ZS) * 2 + x_hi
    down = ((z + ZS - 1) % ZS) * 2 + x_hi
    blocks = ((4, 5, 6, 7), (4, 3, 2, 1), (3, 2, 1), (5, 6, 7))
    targets = (down, up, up, down)
    firsts = (True, False, True, False)

    def ring(out_ref, in_ref, send_sem, recv_sem, prod_ref, half, offsets):
        def copy_of(chain, step):
            k = offsets[chain] + step
            return pltpu.make_async_remote_copy(
                out_ref.at[k],
                in_ref.at[k],
                send_sem,
                recv_sem.at[k],
                device_id={"tp": targets[chain]},
                device_id_type=MESH,
            )

        def sum_at(chain, step):
            rows = slice(0, half) if firsts[chain] else slice(half, 2 * half)
            own = prod_ref[blocks[chain][step], rows, :]
            if step > 0:
                copy_of(chain, step - 1).wait_recv()
                own = own + in_ref[offsets[chain] + step - 1].astype(F32)
            return own

        def step_of(chain, step):
            out_ref[offsets[chain] + step] = sum_at(chain, step).astype(BF16)
            copy_of(chain, step).start()

        def arrived_at(chain, step):
            copy_of(chain, step).wait_recv()
            return in_ref[offsets[chain] + step].astype(F32)

        return step_of, sum_at, arrived_at

    def own_side(block):
        left, right = block[:, 0:128], block[:, 128:256]
        return jnp.where(x_hi == 0, left, right), jnp.where(x_hi == 0, right, left)

    text_step, _, text_arrived = ring(ring_out, ring_in, ring_send, ring_recv, prod, HALF, (0, 4, 8, 11))
    slot_step, slot_at, _ = ring(slot_out, slot_in, slot_send, slot_recv, slot_prod, SLOTS // 2, (0, 3, 6, 8))

    def end_copy(k, count, peer):
        where = pl.ds(k, count)
        return pltpu.make_async_remote_copy(
            end_out.at[where], end_in.at[where], end_send, end_recv, device_id={"tp": peer}, device_id_type=MESH
        )

    def slot_last(chain):
        same, away = own_side(slot_at(chain, len(blocks[chain]) - 1))
        end_out[2 * chain] = same.astype(BF16)
        end_out[2 * chain + 1] = away.astype(BF16)
        end_copy(2 * chain, 1, targets[chain]).start()
        end_copy(2 * chain + 1, 1, targets[chain] + 1 - 2 * x_hi).start()

    project(4)
    project(3)
    project(5)

    for chain in range(4):
        text_step(chain, 0)
    for o in (2, 6, 1, 7, 0):
        project(o)

    part_copy.wait_recv()
    image = (own_sum[...] + dot(slots_b, part_in[...]) + bias_ref[...]).astype(BF16)
    image_rows[...] = image

    def exchange(out_ref, in_ref, send_sem, recv_sem):
        def start(i, _):
            peer = (lane + 1 + (i + 15) % 31) % LANES
            pltpu.make_async_remote_copy(
                out_ref.at[peer], in_ref.at[lane], send_sem, recv_sem, device_id={"lane": peer}, device_id_type=MESH
            ).start()
            return 0

        lax.fori_loop(0, LANES - 1, start, 0, unroll=True)
        in_ref[lane] = out_ref[lane]
        every = pl.ds(0, LANES - 1)
        whole = pltpu.make_async_remote_copy(
            out_ref.at[every],
            in_ref.at[every],
            send_sem,
            recv_sem,
            device_id={"lane": (lane + 1) % LANES},
            device_id_type=MESH,
        )
        return whole.wait_recv, whole.wait_send

    chunk_out[...] = to_chunks(image)
    lane_arrived, lane_sent = exchange(chunk_out, chunk_in, lane_send, lane_recv)

    load_kvg.wait()
    normed_grad = dot_t(kvg[...], kvw[...])
    grad[...] = normed_grad
    place_t = jnp.transpose(place).astype(BF16)
    back_out[...] = to_chunks(dot(place_t, normed_grad.astype(BF16)).astype(BF16))
    back_arrived, back_sent = exchange(back_out, back_in, back_send, back_recv)

    for chain in range(4):
        text_step(chain, 1)
    for chain in range(4):
        if len(blocks[chain]) > 2:
            text_step(chain, 2)

    lane_arrived()
    arrived = from_chunks(chunk_in[...])
    slot_xg[...] = (arrived.astype(F32) * gain).astype(BF16)

    def slot_project(o):
        slot_prod[o] = dot(slot_xg[...], columns(o))

    slot_project(4)
    slot_step(0, 0)
    slot_step(1, 0)
    slot_project(3)
    slot_step(2, 0)
    slot_project(5)
    slot_step(3, 0)
    text_step(0, 3)
    text_step(1, 3)
    for o in (2, 6, 1, 7, 0):
        slot_project(o)
    for chain in range(4):
        slot_step(chain, 1)
    placed = dot(place.astype(BF16), arrived)
    wide = jnp.where(is_image, placed, text[...].astype(F32))
    stream[...] = wide
    squares = jnp.sum(wide * wide, axis=1, keepdims=True)
    dots = jnp.sum(wide * gain * grad[...], axis=1, keepdims=True)
    first = iota((TOKENS, 128), 1) == 0
    both = jnp.transpose(jnp.where(first, squares, dots))
    stat_out[:, 0:TOKENS] = both[0:2, :]

    back_arrived()
    grad_rows[...] = from_chunks(back_in[...])
    rows_wide = image_rows[...].astype(F32)
    row_squares = jnp.sum(rows_wide * rows_wide, axis=1, keepdims=True)
    row_dots = jnp.sum(rows_wide * gain * grad_rows[...].astype(F32), axis=1, keepdims=True)
    row_both = jnp.transpose(jnp.where(iota((SLOTS, 128), 1) == 0, row_squares, row_dots))
    stat_out[:, TOKENS:] = row_both[0:2, :]
    stat_in[tp] = stat_out[...]

    def stat_start(i, _):
        pltpu.make_async_remote_copy(
            stat_out,
            stat_in.at[tp],
            stat_send,
            stat_recv,
            device_id={"tp": (tp + 1 + (i + 7) % 15) % TPS},
            device_id_type=MESH,
        ).start()
        return 0

    lax.fori_loop(0, TPS - 1, stat_start, 0, unroll=True)

    slot_kept, slot_away = own_side(slot_prod[0])
    end_out[8] = slot_away[0 : SLOTS // 2].astype(BF16)
    end_out[9] = slot_away[SLOTS // 2 :].astype(BF16)
    across = z * 2 + (1 - x_hi)
    end_copy(8, 2, across).start()

    text_first = prod[0, 0:HALF, :] + text_arrived(2, 2)
    text_last = prod[0, HALF:TOKENS, :] + text_arrived(3, 2)
    text_first = text_first + text_arrived(0, 3)
    text_last = text_last + text_arrived(1, 3)
    text_kept, text_away = own_side(jnp.concatenate([text_first, text_last], axis=0))
    cross_out[...] = text_away.astype(BF16)
    text_cross = pltpu.make_async_remote_copy(
        cross_out, cross_in, cross_send, cross_recv, device_id={"tp": across}, device_id_type=MESH
    )
    text_cross.start()

    slot_step(0, 2)
    slot_step(1, 2)
    slot_last(2)
    slot_last(3)
    slot_last(0)
    slot_last(1)

    each = pl.ds(0, TPS - 1)
    stat_whole = pltpu.make_async_remote_copy(
        stat_in.at[each], stat_in.at[each], stat_send, stat_recv, device_id={"tp": across}, device_id_type=MESH
    )
    stat_whole.wait_recv()
    totals = jnp.sum(stat_in[...], axis=0)
    inv_row = lax.rsqrt(totals[0:1, :] / D + EPSILON)

    def gradient(where, count, wide, grads):
        inv = jnp.transpose(jnp.broadcast_to(inv_row[:, where], (128, count)))
        total_dots = jnp.transpose(jnp.broadcast_to(totals[1:2, where], (128, count)))
        factor = inv * inv * inv * total_dots / D
        inv4 = jnp.concatenate([inv] * 4, axis=1)
        factor4 = jnp.concatenate([factor] * 4, axis=1)
        return inv, (inv4 * gain * grads - wide * factor4).astype(BF16)

    inv, embed_out[...] = gradient(slice(0, TOKENS), TOKENS, stream[...], grad[...])
    _, row_grad = gradient(
        slice(TOKENS, TOKENS + SLOTS), SLOTS, image_rows[...].astype(F32), grad_rows[...].astype(F32)
    )
    image_out[...] = dot(jnp.transpose(slots).astype(BF16), row_grad).astype(BF16)

    text_cross.wait_recv()
    text_sum = text_kept + cross_in[...].astype(F32)
    every_end = pltpu.make_async_remote_copy(
        end_out, end_in, end_send, end_recv, device_id={"tp": across}, device_id_type=MESH
    )
    every_end.wait_recv()

    def ends(up_or_down, own):
        total = None
        for k in up_or_down:
            part = end_in[k].astype(F32)
            total = part if total is None else total + part
        return total + own

    slot_sum = jnp.concatenate(
        [
            ends((0, 1, 4, 5, 8), slot_kept[0 : SLOTS // 2]),
            ends((2, 3, 6, 7, 9), slot_kept[SLOTS // 2 :]),
        ],
        axis=0,
    )
    high = slot_sum.astype(BF16)
    low = (slot_sum - high.astype(F32)).astype(BF16)
    place_b = place.astype(BF16)
    slot_placed = dot(place_b, high) + dot(place_b, low)
    kv_out[...] = (inv * jnp.where(is_image, slot_placed, text_sum)).astype(BF16)

    part_copy.wait_send()
    lane_sent()
    back_sent()
    stat_whole.wait_send()
    for out_ref, sem, count in ((ring_out, ring_send, 14), (slot_out, slot_send, 10)):
        sent = out_ref.at[pl.ds(0, count)]
        pltpu.make_async_remote_copy(
            sent, sent, sem, sem, device_id={"tp": across}, device_id_type=MESH
        ).wait_send()
    every_end.wait_send()
    text_cross.wait_send()


def finish(kv, embed, image, kv_hbm, embed_hbm, image_hbm, sems):
    copies = []
    for k, (src, dst) in enumerate(((embed, embed_hbm), (image, image_hbm), (kv, kv_hbm))):
        copy = pltpu.make_async_copy(src, dst, sems.at[k])
        copy.start()
        copies.append(copy)
    for copy in copies:
        copy.wait()


def on_device(
    merge_hidden,
    merge_weight,
    merge_bias,
    row_dest,
    image_pos,
    text_embed,
    norm_gain,
    kv_weight,
    kv_grad,
):
    any_space = pl.BlockSpec(memory_space=pl.ANY)
    vmem = pl.BlockSpec(memory_space=pltpu.VMEM)
    dma = pltpu.SemaphoreType.DMA
    shapes = ((TOKENS, KV2 // TPS), (TOKENS, WIDTH), (ROWS, WIDTH))
    results = pl.pallas_call(
        kernel,
        name="step",
        out_shape=tuple(pltpu.VMEM(shape, BF16) for shape in shapes),
        in_specs=[any_space] * 9,
        out_specs=(vmem, vmem, vmem),
        scratch_shapes=[
            pltpu.VMEM((2, ROWS, VD_DEV), BF16),
            pltpu.VMEM((VD_DEV, WIDTH), BF16),
            pltpu.VMEM((1, WIDTH), F32),
            pltpu.VMEM((1, ROWS), jnp.int32),
            pltpu.VMEM((CAP, LANES), jnp.int32),
            pltpu.VMEM((TOKENS, WIDTH), BF16),
            pltpu.VMEM((1, WIDTH), F32),
            pltpu.VMEM((WIDTH, KV2), BF16),
            pltpu.VMEM((TOKENS, KV2), BF16),
            pltpu.VMEM((SLOTS, WIDTH), F32),
            pltpu.VMEM((ROWS, WIDTH), BF16),
            pltpu.VMEM((ROWS, WIDTH), BF16),
            pltpu.VMEM((TOKENS, WIDTH), F32),
            pltpu.VMEM((TOKENS, WIDTH), F32),
            pltpu.VMEM((LANES, 16, 128), BF16),
            pltpu.VMEM((LANES, 16, 128), BF16),
            pltpu.VMEM((SLOTS, WIDTH), BF16),
            pltpu.VMEM((SLOTS, WIDTH), BF16),
            pltpu.VMEM((LANES, 16, 128), BF16),
            pltpu.VMEM((LANES, 16, 128), BF16),
            pltpu.VMEM((2, TOKENS + SLOTS), F32),
            pltpu.VMEM((TPS, 2, TOKENS + SLOTS), F32),
            pltpu.VMEM((TOKENS, WIDTH), BF16),
            pltpu.VMEM((ZS, TOKENS, 256), F32),
            pltpu.VMEM((14, HALF, 256), BF16),
            pltpu.VMEM((14, HALF, 256), BF16),
            pltpu.VMEM((SLOTS, WIDTH), BF16),
            pltpu.VMEM((ZS, SLOTS, 256), F32),
            pltpu.VMEM((10, SLOTS // 2, 256), BF16),
            pltpu.VMEM((10, SLOTS // 2, 256), BF16),
            pltpu.VMEM((TOKENS, 128), BF16),
            pltpu.VMEM((TOKENS, 128), BF16),
            pltpu.VMEM((10, SLOTS // 2, 128), BF16),
            pltpu.VMEM((10, SLOTS // 2, 128), BF16),
            dma((10,)),
            pltpu.SemaphoreType.DMA,
            pltpu.SemaphoreType.DMA,
            pltpu.SemaphoreType.DMA,
            pltpu.SemaphoreType.DMA,
            pltpu.SemaphoreType.DMA,
            pltpu.SemaphoreType.DMA,
            pltpu.SemaphoreType.DMA,
            pltpu.SemaphoreType.DMA,
            pltpu.SemaphoreType.DMA,
            dma((14,)),
            pltpu.SemaphoreType.DMA,
            dma((10,)),
            pltpu.SemaphoreType.DMA,
            pltpu.SemaphoreType.DMA,
            pltpu.SemaphoreType.DMA,
            pltpu.SemaphoreType.DMA,
        ],
        compiler_params=pltpu.CompilerParams(
            collective_id=0, has_side_effects=True, vmem_limit_bytes=65011712
        ),
    )(
        merge_hidden,
        merge_weight,
        merge_bias.reshape(1, WIDTH),
        row_dest.reshape(1, ROWS),
        jnp.transpose(image_pos.reshape(LANES, CAP)),
        text_embed,
        norm_gain.reshape(1, WIDTH),
        kv_weight,
        kv_grad,
    )
    return pl.pallas_call(
        finish,
        name="finish",
        out_shape=tuple(jax.ShapeDtypeStruct(shape, BF16) for shape in shapes),
        in_specs=[vmem] * 3,
        out_specs=(any_space,) * 3,
        scratch_shapes=[dma((3,))],
        compiler_params=pltpu.CompilerParams(vmem_limit_bytes=4 * 1024 * 1024),
    )(*results)


def solution(mesh):
    in_specs = (
        P("lane", "section"),
        P("section", "tp"),
        P("tp"),
        P(("lane", "section")),
        P("lane", "section", None, None),
        P(("lane", "section"), "tp"),
        P("tp"),
        P("tp", None),
        P(("lane", "section"), None),
    )
    out_specs = (
        P(("lane", "section"), "tp"),
        P(("lane", "section"), "tp"),
        P(("lane", "section"), "tp"),
    )
    return jax.shard_map(on_device, mesh=mesh, in_specs=in_specs, out_specs=out_specs, check_vma=False)
```
